512 devices in a mesh: pitch: 32 (over x, z), span: 8 (over y), row: 2 (over core).
Axes of the slice: x: 4, y: 8, z: 8, core: 2. Of those that a mesh axis runs over, the one named last changes fastest.
Arguments:
- fields: float32 [3, 512, 128, 512], P(None, 'pitch', 'span', 'row'), may hold values from -6 to 6
- diffusivity: float32 [512, 128, 512], P('pitch', 'span', 'row'), may hold values from 0.01 to 0.1
- mean_flow: bfloat16 [128, 2, 512], P('span', None, 'row'), may hold values from -6 to 6
- radial_kernel: bfloat16 [128, 128], replicated
- tracer_values: float32 [10, 1048576], P(None, ('pitch', 'span', 'row')), may hold values from -6 to 6
- tracer_cells: int32 [1048576], P(('pitch', 'span', 'row')), may hold values from 0 to 65535
- tracer_dest: int32 [1048576, 1], P(('pitch', 'span', 'row')), may hold values from 0 to 31; in each aligned block of 2048 rows (0 to 2047, 2048 to 4095, ...) at most 128 rows name the same one
- interface_map: int32 [2, 512], P('row', 'pitch'), may hold values from 0 to 511, as said below
Outputs:
- advected: float32 [3, 512, 128, 512], P(None, 'pitch', 'span', 'row')
- arrived: float32 [10, 2097152], P(None, ('pitch', 'span', 'row'))
The draws below stay inside these ranges and needn't reach their ends.
Inputs may be any that keep to these rules, and one draw needn't show every extreme that they name: `tracer_cells`: the local index of the owning cell within the block of the device that holds the tracer, i * 16 * 256 + r * 256 + a for local indices i, r, a. `tracer_dest`: at most 128 of the tracers of one device go to one pitch index. `interface_map`: for one offset o of each draw, row 0 holds (i + o) mod 512 and row 1 holds (i - o) mod 512, so the two rows are inverse permutations.
All inputs are finite; a program needn't handle non-finite values.
Results may differ from the reference program's by a relative error of at most 0.0015.
Values may be sent and summed in bfloat16 or wider, within the bound.
A program may use at most 128 MiB of HBM per device.

```python
import math
import jax
import jax.numpy as jnp
import numpy as np

CP = 16
CR = 16
CA = 256
TRACERS_DEV = 2048
FIELDS = 3
TRACER_VALUES = 10
SUB = 2
NPITCH = 512
NR = 128
NA = 512
CAP = 128
RECV = 4096
TRACERS = 1048576
N_PITCH = 32
N_SPAN = 8
N_ROW = 2
DEVICES = 512


def draw_radial_kernel(key, part):
    index_rows = jnp.arange(NR, dtype=jnp.int32)
    identity = (index_rows[:, None] == index_rows[None, :]).astype(jnp.float32)
    noise = jax.random.normal(key, (NR, NR), jnp.float32)
    return (0.7 * identity + 0.7 * noise / math.sqrt(NR)).astype(jnp.bfloat16)


def draw_interface_map(key, part):
    block_key, cell_key = jax.random.split(jax.random.fold_in(key, 7))
    block_count = NPITCH // CP
    offset = CP * jax.random.randint(block_key, (), 1, block_count) + jax.random.randint(cell_key, (), 0, CP)
    pitch_index = jnp.arange(NPITCH, dtype=jnp.int32)
    return jnp.stack([(pitch_index + offset) % NPITCH, (pitch_index - offset) % NPITCH]).astype(jnp.int32)


def touch_ends(values, stream_key, smallest, high):
    longest = values.shape.index(max(values.shape))
    spots = []
    for shift in (0, 1):
        where = [jax.random.randint(jax.random.fold_in(stream_key, axis), (), 0, length) for axis, length in enumerate(values.shape)]
        where[longest] = (where[longest] + shift) % values.shape[longest]
        spots.append(tuple(where))
    return values.at[spots[0]].set(smallest).at[spots[1]].set(high)


def shard_levels(key, extent, shards, low, largest):
    loudness = 1.0
    for dim, parts in shards:
        heights = jax.random.uniform(jax.random.fold_in(jax.random.fold_in(key, 6), dim), (parts,), jnp.float32, low / len(shards), largest / len(shards))
        loudness = loudness * jnp.repeat(jnp.exp(heights), extent[dim] // parts).reshape((-1,) + (1,) * (len(extent) - 1 - dim))
    return loudness


def shared_out(key, own, number, rows, number_of, top, most, skew):
    ranking = jax.random.permutation(key, number_of)
    heavy_load, ordinary = portions_of(number_of, rows * top, most, skew, True), portions_of(number_of, rows * top, most, skew, False)
    places = jnp.arange(number_of)

    def named(sizes, offset_by):
        used = int((sizes > 0).sum())
        fixed = max(1, used // 4)
        passed = fixed + (places - fixed + offset_by * (used - fixed)) % max(1, number_of - fixed)
        return jnp.zeros((number_of,), jnp.int32).at[ranking[jnp.where(places < fixed, places, passed)]].set(jnp.asarray(sizes, jnp.int32))

    sizes = jnp.where(number % 4 == 0, named(heavy_load, number // 4), named(ordinary, number - number // 4 - 1))
    mixed = jax.random.permutation(jax.random.fold_in(own, 3), number_of)
    source_of, receiver = mixed[0:number_of // 2 * 2:2], mixed[1:number_of // 2 * 2:2]
    room = jnp.minimum(sizes[source_of] - 1, most - sizes[receiver]) // 2
    room = jnp.where((source_of == ranking[0]) | (receiver == ranking[0]) | (sizes[receiver] == 0), 0, jnp.maximum(room, 0))
    passed = jax.random.randint(jax.random.fold_in(own, 4), (number_of // 2,), 0, 1 << 20) % (room + 1)
    sizes = sizes.at[source_of].add(-passed).at[receiver].add(passed)
    members = jnp.searchsorted(jnp.cumsum(sizes), jnp.arange(rows * top), side="right").astype(jnp.int32)
    table = members.reshape(top, rows).T
    table = table[jax.random.permutation(jax.random.fold_in(own, 1), rows)]
    offset_by = jax.random.randint(jax.random.fold_in(own, 2), (rows, 1), 0, top)
    return jnp.take_along_axis(table, (jnp.arange(top)[None, :] + offset_by) % top, axis=1)


def portions_of(number_of, total, reach, skew, full):
    weights = [(1 << 20) // math.isqrt(rank ** skew) + 1 for rank in range(1, number_of + 1)]
    largest = reach if full else min(reach, max(-(-total // number_of), total * weights[0] // sum(weights)))
    least = 1 if total - largest >= number_of - 1 else 0
    counts, rest = [largest] + [least] * (number_of - 1), total - largest - least * (number_of - 1)
    while rest > 0:
        free = [i for i in range(1, number_of) if counts[i] < largest] or [i for i in range(1, number_of) if counts[i] < reach]
        mass, remaining = sum([weights[i] for i in free]), rest
        for i in free:
            extra = min(reach - counts[i], max(1, remaining * weights[i] // mass), rest)
            counts[i] = counts[i] + extra
            rest = rest - extra
    return np.array(counts)


def gaussian(key, shape, scale, limit, shards=(), held_as=jnp.bfloat16):
    entries = scale * jax.random.normal(key, shape, jnp.float32)
    if shards:
        entries = entries * shard_levels(key, shape, shards, -0.22, 0.18)
    return jnp.clip(entries, -limit, limit).astype(held_as)


def setup_inputs(seed: int = 0) -> dict:
    splits = jax.random.split(jax.random.key(seed), 9)
    fields = gaussian(splits[0], (FIELDS, NPITCH, NR, NA), 1.0, 6.0, ((1, 32), (2, 8), (3, 2)), jnp.float32)
    diffusivity = jnp.clip(jnp.exp(math.log(0.1) - 2.3025851 * jax.random.uniform(splits[1], (NPITCH, NR, NA), jnp.float32) ** shard_levels(splits[1], (NPITCH, NR, NA), ((0, 32), (1, 8), (2, 2)), -0.2, 0.2)), 0.01, 0.1)
    mean_flow = gaussian(splits[2], (NR, 2, NA), 1.0, 6.0, ((0, 8), (2, 2)))
    radial_kernel = draw_radial_kernel(jax.random.fold_in(splits[8], 71), 0)
    tracer_values = gaussian(splits[4], (TRACER_VALUES, TRACERS), 1.0, 6.0, ((1, 512),), jnp.float32)
    tracer_cells = touch_ends(jax.random.randint(splits[5], (TRACERS,), 0, CP * CR * CA), jax.random.fold_in(splits[5], 1), 0, (CP * CR * CA) - 1).astype(jnp.int32)
    tracer_dest_keys = jax.random.split(jax.random.fold_in(splits[6], 1), TRACERS // TRACERS_DEV)
    tracer_dest_turns = jax.random.permutation(jax.random.fold_in(splits[6], 3), TRACERS // TRACERS_DEV)
    tracer_dest = jax.vmap(lambda own, number: shared_out(jax.random.fold_in(splits[6], 2), own, number, TRACERS_DEV, N_PITCH, 1, CAP, 2))(tracer_dest_keys, tracer_dest_turns).reshape((TRACERS, 1))
    interface_map = draw_interface_map(jax.random.fold_in(splits[8], 71), 0)
    return dict(fields=fields, diffusivity=diffusivity, mean_flow=mean_flow, radial_kernel=radial_kernel, tracer_values=tracer_values, tracer_cells=tracer_cells, tracer_dest=tracer_dest, interface_map=interface_map)


TIME_STEP = 0.9
AXIAL_SPEED = 0.15
PITCH_SPEED = 0.15


def face_flux(left_values, right_values, left_kappa, right_kappa, face_speed):
    diffusion = -0.5 * (left_kappa + right_kappa) * (right_values - left_values)
    if face_speed is None:
        return diffusion
    return jnp.maximum(face_speed, 0.0) * left_values + jnp.minimum(face_speed, 0.0) * right_values + diffusion


def axial_line(array, ghost, row_number):
    upstream = (array[..., 0], ghost)[row_number]
    downstream = (ghost, array[..., -1])[row_number]
    return jnp.concatenate([upstream[..., None], array, downstream[..., None]], -1)


def advance_field(values, kappa, speed_axial, speed_pitch, ghost_values, ghost_kappa, ghost_speed, row_number):
    pitch_values = jnp.concatenate([values[-1:], values, values[:1]], 0)
    pitch_kappa = jnp.concatenate([kappa[-1:], kappa, kappa[:1]], 0)
    pitch_flux = face_flux(pitch_values[:-1], pitch_values[1:], pitch_kappa[:-1], pitch_kappa[1:], speed_pitch)
    radial_values = jnp.pad(values, ((0, 0), (1, 1), (0, 0)))
    radial_kappa = jnp.pad(kappa, ((0, 0), (1, 1), (0, 0)))
    face_index = jnp.arange(NR + 1, dtype=jnp.int32)
    wall_mask = ((face_index > 0) & (face_index < NR)).astype(jnp.float32)
    radial_flux = face_flux(radial_values[:, :-1], radial_values[:, 1:], radial_kappa[:, :-1], radial_kappa[:, 1:], None) * wall_mask[:, None]
    speed_full = jnp.broadcast_to(speed_axial[None], values.shape)
    line_values = axial_line(values, ghost_values, row_number)
    line_kappa = axial_line(kappa, ghost_kappa, row_number)
    line_speed = axial_line(speed_full, ghost_speed, row_number)
    face_speed = 0.5 * (line_speed[..., :-1] + line_speed[..., 1:])
    axial_flux = face_flux(line_values[..., :-1], line_values[..., 1:], line_kappa[..., :-1], line_kappa[..., 1:], face_speed)
    divergence = pitch_flux[1:] - pitch_flux[:-1] + radial_flux[:, 1:] - radial_flux[:, :-1] + axial_flux[..., 1:] - axial_flux[..., :-1]
    return values - TIME_STEP * divergence


def reference(fields, diffusivity, mean_flow, radial_kernel, tracer_values, tracer_cells, tracer_dest, interface_map):
    smoothed = jnp.dot(radial_kernel, mean_flow.reshape(NR, 2 * NA), preferred_element_type=jnp.float32).reshape(NR, 2, NA)
    speed_axial = AXIAL_SPEED * (1.0 + 0.5 * jnp.tanh(smoothed[:, 0]))
    speed_pitch = PITCH_SPEED * jnp.tanh(smoothed[:, 1])

    tracer_ids = jnp.arange(TRACERS, dtype=jnp.int32)
    device_ids = tracer_ids // TRACERS_DEV
    pitch_dev = device_ids // (N_SPAN * N_ROW)
    span_dev = (device_ids // N_ROW) % N_SPAN
    row_dev = device_ids % N_ROW
    global_pitch = pitch_dev * CP + tracer_cells // (CR * CA)
    global_radial = span_dev * CR + (tracer_cells // CA) % CR
    global_axial = row_dev * CA + tracer_cells % CA
    sample_fields = fields[:, global_pitch, global_radial, global_axial]
    sample_speed = jnp.stack([speed_axial[global_radial, global_axial], speed_pitch[global_radial, global_axial]])
    sampled = jnp.concatenate([sample_fields, sample_speed], 0)
    head_rows = tracer_values[:5]
    tail_rows = tracer_values[5:]
    updated = jnp.concatenate([head_rows + 0.5 * (sampled - head_rows), tail_rows + 0.8 * sampled], 0)
    targets = tracer_dest[:, 0]
    onehot = (targets.reshape(DEVICES, TRACERS_DEV)[:, :, None] == jnp.arange(N_PITCH, dtype=jnp.int32)[None, None]).astype(jnp.int32)
    slot_index = jnp.sum((jnp.cumsum(onehot, 1) - onehot) * onehot, 2).reshape(TRACERS)
    position = ((targets * N_SPAN + span_dev) * N_ROW + row_dev) * RECV + pitch_dev * CAP + slot_index
    arrived = jnp.zeros((TRACER_VALUES, DEVICES * RECV), jnp.float32).at[:, position].set(updated)

    current = fields
    for substep in range(SUB):
        plane_values = []
        plane_kappa = []
        plane_speed = []
        for row_number in range(2):
            plane = row_number * CA + (CA - 1) * (1 - row_number)
            plane_values.append(current[:, :, :, plane])
            plane_kappa.append(diffusivity[:, :, plane])
            plane_speed.append(jnp.broadcast_to(speed_axial[None, :, plane], (NPITCH, NR)))
        new_rows = []
        for row_number in range(2):
            other_row = 1 - row_number
            facing = interface_map[row_number]
            ghost_values = plane_values[other_row][:, facing, :]
            ghost_kappa = plane_kappa[other_row][facing, :]
            ghost_speed = plane_speed[other_row][facing, :]
            first_cell = row_number * CA
            kappa_row = diffusivity[:, :, first_cell:first_cell + CA]
            axial_row = speed_axial[:, first_cell:first_cell + CA]
            pitch_row = speed_pitch[:, first_cell:first_cell + CA]
            advanced = []
            for field_number in range(FIELDS):
                advanced.append(advance_field(current[field_number, :, :, first_cell:first_cell + CA], kappa_row, axial_row, pitch_row, ghost_values[field_number], ghost_kappa, ghost_speed, row_number))
            new_rows.append(jnp.stack(advanced))
        current = jnp.concatenate(new_rows, -1)
    return current, arrived
```

```python
import functools

import jax
import jax.numpy as jnp
from jax import lax
from jax.experimental import pallas as pl
from jax.experimental.pallas import tpu as pltpu
from jax.sharding import PartitionSpec as P

TIME_STEP = 0.9
AXIAL_SPEED = 0.15
PITCH_SPEED = 0.15
CHUNK = 256
MESH = pl.DeviceIdType.MESH
F32 = jnp.float32
BF16 = jnp.bfloat16


def iota(shape, dim):
    return lax.broadcasted_iota(jnp.int32, shape, dim)


def halves(x):
    high = x.astype(BF16)
    return high, (x - high.astype(F32)).astype(BF16)


def dot(a, b):
    return jnp.dot(a, b, preferred_element_type=F32)


def dot_nt(a, b):
    return lax.dot_general(a, b, (((1,), (1,)), ((), ())), preferred_element_type=F32)


def kernel(
    npitch,
    nspan,
    fields_hbm,
    kappa_hbm,
    flow_hbm,
    radial_hbm,
    values_hbm,
    cells_hbm,
    dest_hbm,
    map_ref,
    advected_ref,
    arrived_ref,
    state,
    flow_raw,
    radial,
    values,
    cells,
    dest,
    flow_own,
    flows,
    state2,
    span_send,
    span_recv,
    plane_send,
    planes_first,
    planes_second,
    speed_send,
    speed_recv,
    outgoing,
    landed,
    fparts,
    sampled,
    slots,
    counts,
    hand,
    speeds,
    coef,
    ghosts,
    load_sem,
    flow_sems,
    pitch_sems,
    span_sems,
    plane_sems,
    speed_sems,
    hand_sems,
):
    p = lax.axis_index("pitch")
    s = lax.axis_index("span")
    q = lax.axis_index("row")
    other = 1 - q
    cp, cr, ca = 16, 16, 256
    tracers = values.shape[1]
    nchunk = tracers // CHUNK

    loads = [
        pltpu.make_async_copy(flow_hbm, flow_raw, load_sem.at[0]),
        pltpu.make_async_copy(dest_hbm, dest, load_sem.at[1]),
        pltpu.make_async_copy(fields_hbm, state.at[0:3, 1 : cp + 1], load_sem.at[2]),
        pltpu.make_async_copy(kappa_hbm, state.at[3, 1 : cp + 1], load_sem.at[3]),
        pltpu.make_async_copy(cells_hbm, cells, load_sem.at[4]),
        pltpu.make_async_copy(radial_hbm, radial, load_sem.at[5]),
        pltpu.make_async_copy(values_hbm, values, load_sem.at[6]),
    ]
    for copy in loads:
        copy.start()

    def wrap(index, count):
        return lax.rem(index, count)

    barrier = pltpu.get_barrier_semaphore()

    @pl.loop(1, npitch)
    def _(step):
        pl.semaphore_signal(barrier, inc=1, device_id=(wrap(p + step, npitch), s, q), device_id_type=MESH)

    @pl.loop(0, npitch)
    def _(step):
        pl.semaphore_signal(barrier, inc=1, device_id=(wrap(p + step, npitch), s, other), device_id_type=MESH)

    @pl.loop(1, nspan)
    def _(step):
        pl.semaphore_signal(barrier, inc=1, device_id=(p, wrap(s + step, nspan), q), device_id_type=MESH)

    loads[0].wait()
    raw = flow_raw[...].astype(F32)
    flow_own[...] = jnp.concatenate([raw[:, 0, :], raw[:, 1, :]], axis=1).astype(BF16)

    lane = iota((8, 128), 1)
    source_lane = 127 * other
    near = lax.rem(lane + 128 - source_lane, 128)
    offset = pl.multiple_of(other * 128, 128)

    def pack(tiles):
        def body(i, packed):
            packed = pltpu.roll(packed, 127, 1)
            for f in range(4):
                for half in range(2):
                    group = f * 2 + half
                    tile = tiles(f, i, half)
                    spot = group * 16 + 15
                    packed = jnp.where(near == spot, pltpu.roll(tile, spot, 1), packed)
            return packed

        packed = lax.fori_loop(0, cp, body, jnp.zeros((8, 128), F32))
        return jnp.where(q == 0, pltpu.roll(packed, 1, 1), packed)

    loads[2].wait()
    loads[3].wait()
    plane_send[0] = pack(lambda f, i, half: state[f, i + 1, pl.ds(half * 8, 8), pl.ds(offset, 128)])

    @pl.loop(0, cp)
    def _(i):
        for f in range(4):
            span_send[0, 0, f, pl.ds(i, 1), :] = state[f, i + 1, 0:1, :]
            span_send[0, 1, f, pl.ds(i, 1), :] = state[f, i + 1, cr - 1 : cr, :]

    pl.semaphore_wait(barrier, 2 * npitch - 1 + nspan - 1)

    @pl.loop(1, nspan)
    def _(step):
        pltpu.make_async_remote_copy(
            src_ref=flow_own,
            dst_ref=flows.at[s],
            send_sem=flow_sems.at[0],
            recv_sem=flow_sems.at[1],
            device_id=(p, wrap(s + step, nspan), q),
            device_id_type=MESH,
        ).start()

    flows[s] = flow_own[...]

    up, down = wrap(p + 1, npitch), wrap(p + npitch - 1, npitch)
    outer, inner = wrap(s + 1, nspan), wrap(s + nspan - 1, nspan)

    def halo(ref, step, count):
        return [
            pltpu.make_async_remote_copy(
                src_ref=ref.at[0:count, cp],
                dst_ref=ref.at[0:count, 0],
                send_sem=pitch_sems.at[step, 0],
                recv_sem=pitch_sems.at[step, 1],
                device_id=(up, s, q),
                device_id_type=MESH,
            ),
            pltpu.make_async_remote_copy(
                src_ref=ref.at[0:count, 1],
                dst_ref=ref.at[0:count, cp + 1],
                send_sem=pitch_sems.at[step, 2],
                recv_sem=pitch_sems.at[step, 3],
                device_id=(down, s, q),
                device_id_type=MESH,
            ),
            pltpu.make_async_remote_copy(
                src_ref=span_send.at[step, 0, 0:count],
                dst_ref=span_recv.at[step, 1, 0:count],
                send_sem=span_sems.at[step, 0],
                recv_sem=span_sems.at[step, 1],
                device_id=(p, inner, q),
                device_id_type=MESH,
            ),
            pltpu.make_async_remote_copy(
                src_ref=span_send.at[step, 1, 0:count],
                dst_ref=span_recv.at[step, 0, 0:count],
                send_sem=span_sems.at[step, 2],
                recv_sem=span_sems.at[step, 3],
                device_id=(p, outer, q),
                device_id_type=MESH,
            ),
        ]

    planes = (planes_first, planes_second)

    def spread_plane(step):
        @pl.loop(0, npitch)
        def _(far):
            pltpu.make_async_remote_copy(
                src_ref=plane_send.at[step],
                dst_ref=planes[step].at[p],
                send_sem=plane_sems.at[step, 0],
                recv_sem=plane_sems.at[step, 1],
                device_id=(wrap(p + far, npitch), s, other),
                device_id_type=MESH,
            ).start()

    def wait_plane(step):
        pltpu.make_async_copy(planes[step], planes[step], plane_sems.at[step, 0]).wait()
        pltpu.make_async_copy(planes[step], planes[step], plane_sems.at[step, 1]).wait()

    first = halo(state, 0, 4)
    for copy in first:
        copy.start()
    spread_plane(0)

    for f in range(3):
        block = state[f, 1 : cp + 1].reshape(cp * cr, ca)
        high, low = halves(block)
        fparts[0, f] = high
        fparts[1, f] = low
    loads[1].wait()
    loads[4].wait()
    counts[...] = jnp.zeros((npitch, 1), F32)
    before = (iota((CHUNK, CHUNK), 0) < iota((CHUNK, CHUNK), 1)).astype(F32).astype(BF16)

    @pl.loop(0, nchunk)
    def _(chunk):
        here = pl.ds(pl.multiple_of(chunk * CHUNK, CHUNK), CHUNK)
        cell = cells[0:1, here]
        axial = lax.bitwise_and(cell, ca - 1)
        place = lax.shift_right_logical(cell, 8)
        onehot = (iota((ca, CHUNK), 0) == axial).astype(F32).astype(BF16)
        at_place = iota((cp * cr, CHUNK), 0) == place
        for f in range(3):
            picked = dot(fparts[0, f], onehot) + dot(fparts[1, f], onehot)
            sampled[f : f + 1, here] = jnp.sum(jnp.where(at_place, picked, 0.0), axis=0, keepdims=True)
        goal = dest[0:1, here]
        mine = iota((npitch, CHUNK), 0) == goal
        mine_f = mine.astype(F32)
        rank = dot(mine_f.astype(BF16), before) + counts[...]
        slots[0:1, here] = jnp.sum(jnp.where(mine, rank, 0.0), axis=0, keepdims=True)
        counts[...] += jnp.sum(mine_f, axis=1, keepdims=True)

    some = flows.at[0 : nspan - 1]
    pltpu.make_async_copy(some, some, flow_sems.at[0]).wait()
    pltpu.make_async_copy(some, some, flow_sems.at[1]).wait()

    loads[5].wait()
    kernel_rows = radial[pl.ds(pl.multiple_of(s * cr, cr), cr), :]
    smoothed = dot(kernel_rows, flows[...].reshape(nspan * cr, 2 * ca))
    speed_axial = AXIAL_SPEED * (1.0 + 0.5 * jnp.tanh(smoothed[:, :ca]))
    speed_pitch = PITCH_SPEED * jnp.tanh(smoothed[:, ca:])
    speeds[0] = speed_axial
    speeds[1] = speed_pitch
    edge = jnp.where(q == 0, speed_axial[:, ca - 1 : ca], speed_axial[:, 0:1])
    speed_send[...] = jnp.broadcast_to(edge, (cr, 128))
    speed_copy = pltpu.make_async_remote_copy(
        src_ref=speed_send,
        dst_ref=speed_recv,
        send_sem=speed_sems.at[0],
        recv_sem=speed_sems.at[1],
        device_id=(p, s, other),
        device_id_type=MESH,
    )
    speed_copy.start()

    loads[6].wait()
    hand[...] = jnp.zeros(hand.shape, F32)
    speed_parts = halves(speeds[...].reshape(2 * cr, ca))

    @pl.loop(0, nchunk)
    def _(chunk):
        here = pl.ds(pl.multiple_of(chunk * CHUNK, CHUNK), CHUNK)
        cell = cells[0:1, here]
        axial = lax.bitwise_and(cell, ca - 1)
        onehot = (iota((ca, CHUNK), 0) == axial).astype(F32).astype(BF16)
        picked = dot(speed_parts[0], onehot) + dot(speed_parts[1], onehot)
        radius = lax.bitwise_and(lax.shift_right_logical(cell, 8), cr - 1)
        at_radius = iota((cr, CHUNK), 0) == radius
        got = [sampled[f : f + 1, here] for f in range(3)]
        for k in range(2):
            got.append(jnp.sum(jnp.where(at_radius, picked[k * cr : (k + 1) * cr], 0.0), axis=0, keepdims=True))
        which = iota((16, CHUNK), 0)
        item = jnp.where(which >= 5, which - 5, which)
        samples = jnp.zeros((16, CHUNK), F32)
        for k in range(5):
            samples = jnp.where(item == k, got[k], samples)
        old = jnp.concatenate([values[:, here], jnp.zeros((6, CHUNK), F32)], axis=0)
        updated = jnp.where(which < 5, old + 0.5 * (samples - old), old + 0.8 * samples)
        high, low = halves(updated)
        slot = slots[0:1, here].astype(jnp.int32)
        slot_hot = (iota((128, CHUNK), 0) == slot).astype(F32).astype(BF16)
        goal = jnp.broadcast_to(dest[0:1, here], (16, CHUNK))
        zero = jnp.zeros((16, CHUNK), F32)
        masks = [goal == d for d in range(npitch)]
        left = jnp.concatenate([jnp.where(m, high.astype(F32), zero).astype(BF16) for m in masks], axis=0)
        hand[...] += dot_nt(left, slot_hot)
        left = jnp.concatenate([jnp.where(m, low.astype(F32), zero).astype(BF16) for m in masks], axis=0)
        hand[...] += dot_nt(left, slot_hot)

    for d in range(npitch):
        outgoing[d] = hand[d * 16 : d * 16 + 10, :]

    @pl.loop(1, npitch)
    def _(step):
        to = wrap(p + step, npitch)
        pltpu.make_async_remote_copy(
            src_ref=outgoing.at[to],
            dst_ref=landed.at[p],
            send_sem=hand_sems.at[0],
            recv_sem=hand_sems.at[1],
            device_id=(to, s, q),
            device_id_type=MESH,
        ).start()

    landed[p] = outgoing[p]

    for copy in first:
        copy.wait()
    wait_plane(0)
    speed_copy.wait()

    start_cell = map_ref[0, 0]
    facing = lax.shift_right_logical(start_cell, 4)
    shift = lax.bitwise_and(start_cell, 15)
    facing_next = lax.bitwise_and(facing + 1, npitch - 1)
    in_group = lax.bitwise_and(lane, 15)

    def ghost(step, count):
        low = planes[step][facing]
        high = planes[step][facing_next]
        high = pltpu.roll(high, 16, 1)
        for bit in range(4):
            moved = lax.bitwise_and(shift, 1 << bit) != 0
            low = jnp.where(moved, pltpu.roll(low, 128 - (1 << bit), 1), low)
            high = jnp.where(moved, pltpu.roll(high, 128 - (1 << bit), 1), high)
        window = jnp.where(in_group + shift < 16, low, high)

        def body(i, tile):
            for f in range(count):
                for half in range(2):
                    group = f * 2 + half
                    ghosts[f, i, half * 8 : half * 8 + 8, :] = jnp.broadcast_to(
                        tile[:, group * 16 : group * 16 + 1], (8, 128)
                    )
            return pltpu.roll(tile, 127, 1)

        lax.fori_loop(0, cp, body, window)

    ghost(0, 4)
    lanes = iota((cr, ca), 1)
    radii = iota((cr, ca), 0)
    west, east = lanes == 0, lanes == ca - 1
    hub, tip = radii == 0, radii == cr - 1
    stator = q == 0
    span_first = s == 0
    span_last = s == nspan - 1

    def twice(x):
        return jnp.concatenate([x, x], axis=1)

    def around(x, inner_row, outer_row, ghost_tile):
        out = jnp.where(tip, outer_row, pltpu.roll(x, cr - 1, 0))
        inn = jnp.where(hub, inner_row, pltpu.roll(x, 1, 0))
        right = jnp.where(east, ghost_tile, pltpu.roll(x, ca - 1, 1))
        left = jnp.where(west, ghost_tile, pltpu.roll(x, 1, 1))
        return out, inn, right, left

    sa = speeds[0]
    sp = speeds[1]
    ghost_speed = twice(speed_recv[...])
    no_west = jnp.logical_and(west, stator)
    no_east = jnp.logical_and(east, jnp.logical_not(stator))
    sa_right = jnp.where(no_east, sa, jnp.where(east, ghost_speed, pltpu.roll(sa, ca - 1, 1)))
    sa_left = jnp.where(no_west, sa, jnp.where(west, ghost_speed, pltpu.roll(sa, 1, 1)))
    w_east = 0.5 * (sa + sa_right)
    w_west = 0.5 * (sa + sa_left)
    ep, em = jnp.maximum(w_east, 0.0), jnp.minimum(w_east, 0.0)
    wp, wm = jnp.maximum(w_west, 0.0), jnp.minimum(w_west, 0.0)
    pp, pm = jnp.maximum(sp, 0.0), jnp.minimum(sp, 0.0)
    no_inner = jnp.logical_and(hub, span_first)
    no_outer = jnp.logical_and(tip, span_last)

    @pl.loop(0, cp)
    def _(i):
        k = state[3, i + 1]
        k_out, k_in, k_right, k_left = around(
            k, span_recv[0, 0, 3, pl.ds(i, 1), :], span_recv[0, 1, 3, pl.ds(i, 1), :], twice(ghosts[3, i])
        )
        k_right = jnp.where(no_east, k, k_right)
        k_left = jnp.where(no_west, k, k_left)
        d_up = 0.5 * (k + state[3, i + 2])
        d_down = 0.5 * (k + state[3, i])
        d_out = jnp.where(no_outer, 0.0, 0.5 * (k + k_out))
        d_in = jnp.where(no_inner, 0.0, 0.5 * (k + k_in))
        d_east = 0.5 * (k + k_right)
        d_west = 0.5 * (k + k_left)
        c_up = TIME_STEP * (d_up - pm)
        c_down = TIME_STEP * (d_down + pp)
        c_out = TIME_STEP * d_out
        c_in = TIME_STEP * d_in
        c_east = TIME_STEP * (d_east - em)
        c_west = TIME_STEP * (d_west + wp)
        center = 1.0 - (c_up + c_down + c_out + c_in) - TIME_STEP * (ep + d_east + d_west - wm)
        center = center + jnp.where(no_east, c_east, 0.0) + jnp.where(no_west, c_west, 0.0)
        coef[0, i] = center
        coef[1, i] = c_up
        coef[2, i] = c_down
        coef[3, i] = c_out
        coef[4, i] = c_in
        coef[5, i] = jnp.where(no_east, 0.0, c_east)
        coef[6, i] = jnp.where(no_west, 0.0, c_west)

    def advance(old, step, store):
        @pl.loop(0, cp)
        def _(i):
            c = [coef[n, i] for n in range(7)]
            for f in range(3):
                v = old[f, i + 1]
                out, inn, right, left = around(
                    v, span_recv[step, 0, f, pl.ds(i, 1), :], span_recv[step, 1, f, pl.ds(i, 1), :], twice(ghosts[f, i])
                )
                new = c[0] * v + c[1] * old[f, i + 2] + c[2] * old[f, i]
                new = new + c[3] * out + c[4] * inn + c[5] * right + c[6] * left
                store(f, i, new)

    def store_first(f, i, new):
        state2[f, i + 1] = new
        span_send[1, 0, f, pl.ds(i, 1), :] = new[0:1, :]
        span_send[1, 1, f, pl.ds(i, 1), :] = new[cr - 1 : cr, :]

    advance(state, 0, store_first)

    second = halo(state2, 1, 3)
    for copy in second:
        copy.start()
    plane_send[1] = pack(lambda f, i, half: state2[min(f, 2), i + 1, pl.ds(half * 8, 8), pl.ds(offset, 128)])
    spread_plane(1)
    for copy in second:
        copy.wait()
    wait_plane(1)
    ghost(1, 3)

    def store_second(f, i, new):
        advected_ref[f, i] = new

    advance(state2, 1, store_second)

    many = landed.at[0 : npitch - 1]
    pltpu.make_async_copy(many, many, hand_sems.at[0]).wait()
    pltpu.make_async_copy(many, many, hand_sems.at[1]).wait()

    for d in range(npitch):
        arrived_ref[:, d * 128 : (d + 1) * 128] = landed[d]


def local(fields, diffusivity, mean_flow, radial_kernel, tracer_values, tracer_cells, tracer_dest, interface_map):
    npitch = lax.axis_size("pitch")
    nspan = lax.axis_size("span")
    tracers = tracer_values.shape[1]
    anywhere = pl.BlockSpec(memory_space=pltpu.HBM)
    vmem = pl.BlockSpec(memory_space=pltpu.VMEM)
    dma = pltpu.SemaphoreType.DMA
    return pl.pallas_call(
        functools.partial(kernel, npitch, nspan),
        out_shape=(
            jax.ShapeDtypeStruct((3, 16, 16, 256), F32),
            jax.ShapeDtypeStruct((10, npitch * 128), F32),
        ),
        in_specs=[anywhere] * 7 + [pl.BlockSpec(memory_space=pltpu.SMEM)],
        out_specs=(vmem, vmem),
        scratch_shapes=[
            pltpu.VMEM((4, 18, 16, 256), F32),
            pltpu.VMEM((16, 2, 256), BF16),
            pltpu.VMEM((128, nspan * 16), BF16),
            pltpu.VMEM((10, tracers), F32),
            pltpu.VMEM((1, tracers), jnp.int32),
            pltpu.VMEM((1, tracers), jnp.int32),
            pltpu.VMEM((16, 512), BF16),
            pltpu.VMEM((nspan, 16, 512), BF16),
            pltpu.VMEM((3, 18, 16, 256), F32),
            pltpu.VMEM((2, 2, 4, 16, 256), F32),
            pltpu.VMEM((2, 2, 4, 16, 256), F32),
            pltpu.VMEM((2, 8, 128), F32),
            pltpu.VMEM((npitch, 8, 128), F32),
            pltpu.VMEM((npitch, 8, 128), F32),
            pltpu.VMEM((16, 128), F32),
            pltpu.VMEM((16, 128), F32),
            pltpu.VMEM((npitch, 10, 128), F32),
            pltpu.VMEM((npitch, 10, 128), F32),
            pltpu.VMEM((2, 3, 256, 256), BF16),
            pltpu.VMEM((8, tracers), F32),
            pltpu.VMEM((8, tracers), F32),
            pltpu.VMEM((npitch, 1), F32),
            pltpu.VMEM((npitch * 16, 128), F32),
            pltpu.VMEM((2, 16, 256), F32),
            pltpu.VMEM((7, 16, 16, 256), F32),
            pltpu.VMEM((4, 16, 16, 128), F32),
            dma((7,)),
            dma((2,)),
            dma((2, 4)),
            dma((2, 4)),
            dma((2, 2)),
            dma((2,)),
            dma((2,)),
        ],
        compiler_params=pltpu.CompilerParams(
            collective_id=0, has_side_effects=True, vmem_limit_bytes=60 * 1024 * 1024
        ),
        name="row_step",
    )(
        fields,
        diffusivity,
        mean_flow,
        radial_kernel,
        tracer_values,
        tracer_cells.reshape(1, tracers),
        tracer_dest.reshape(1, tracers),
        interface_map,
    )


def solution(mesh):
    placed = (
        P(None, "pitch", "span", "row"),
        P("pitch", "span", "row"),
        P("span", None, "row"),
        P(),
        P(None, ("pitch", "span", "row")),
        P(("pitch", "span", "row")),
        P(("pitch", "span", "row"), None),
        P("row", "pitch"),
    )
    return jax.shard_map(
        local,
        mesh=mesh,
        in_specs=placed,
        out_specs=(P(None, "pitch", "span", "row"), P(None, ("pitch", "span", "row"))),
        check_vma=False,
    )
```

```python
import functools

import jax
import jax.numpy as jnp
from jax import lax
from jax.experimental import pallas as pl
from jax.experimental.pallas import tpu as pltpu
from jax.sharding import PartitionSpec as P

TIME_STEP = 0.9
AXIAL_SPEED = 0.15
PITCH_SPEED = 0.15
CHUNK = 512
UNROLL = 16
DEEP = 8
MESH = pl.DeviceIdType.MESH
F32 = jnp.float32
BF16 = jnp.bfloat16


def iota(shape, dim):
    return lax.broadcasted_iota(jnp.int32, shape, dim)


def halves(x):
    high = x.astype(BF16)
    return high, (x - high.astype(F32)).astype(BF16)


def dot(a, b):
    return jnp.dot(a, b, preferred_element_type=F32)


def dot_nt(a, b):
    return lax.dot_general(a, b, (((1,), (1,)), ((), ())), preferred_element_type=F32)


def kernel(
    npitch,
    nspan,
    fields_hbm,
    kappa_hbm,
    flow_hbm,
    radial_hbm,
    values_hbm,
    cells_hbm,
    dest_hbm,
    map_ref,
    advected_ref,
    arrived_ref,
    state,
    flow_raw,
    radial,
    values,
    cells,
    dest,
    flow_own,
    flows,
    state2,
    span_send,
    span_recv,
    plane_send,
    plane_in,
    planes_first,
    planes_second,
    speed_send,
    speed_recv,
    outgoing,
    midway,
    landed,
    fparts,
    sampled,
    slots,
    counts,
    hand,
    speeds,
    coef,
    ghosts,
    load_sem,
    flow_sems,
    pitch_sems,
    span_sems,
    plane_sems,
    speed_sems,
    hand_sems,
):
    p = lax.axis_index("pitch")
    s = lax.axis_index("span")
    q = lax.axis_index("row")
    other = 1 - q
    cp, cr, ca = 16, 16, 256
    tracers = values.shape[1]
    nchunk = tracers // CHUNK

    loads = [
        pltpu.make_async_copy(flow_hbm, flow_raw, load_sem.at[0]),
        pltpu.make_async_copy(dest_hbm, dest, load_sem.at[1]),
        pltpu.make_async_copy(fields_hbm, state.at[0:3, 1 : cp + 1], load_sem.at[2]),
        pltpu.make_async_copy(kappa_hbm, state.at[3, 1 : cp + 1], load_sem.at[3]),
        pltpu.make_async_copy(cells_hbm, cells, load_sem.at[4]),
        pltpu.make_async_copy(radial_hbm, radial, load_sem.at[5]),
        pltpu.make_async_copy(values_hbm, values, load_sem.at[6]),
    ]
    for copy in loads:
        copy.start()

    def wrap(index, count):
        return lax.bitwise_and(index, count - 1)

    barrier = pltpu.get_barrier_semaphore()

    wide = npitch // DEEP
    x, z = lax.shift_right_logical(p, 3), lax.bitwise_and(p, DEEP - 1)
    z_peers = [x * DEEP + wrap(z + step, DEEP) for step in range(1, DEEP)]
    x_peers = [wrap(p + step * DEEP, npitch) for step in range(1, wide)]
    span_peers = [wrap(s + step, nspan) for step in range(1, nspan)]
    up, down = wrap(p + 1, npitch), wrap(p + npitch - 1, npitch)
    outer, inner = wrap(s + 1, nspan), wrap(s + nspan - 1, nspan)
    greeted = [(p, s, other), (up, s, q), (down, s, q)]
    greeted += [(p, peer, q) for peer in span_peers]
    greeted += [(peer, s, q) for peer in z_peers + x_peers]
    for device in greeted:
        pl.semaphore_signal(barrier, inc=1, device_id=device, device_id_type=MESH)

    loads[0].wait()
    raw = flow_raw[...].astype(F32)
    flow_own[...] = jnp.concatenate([raw[:, 0, :], raw[:, 1, :]], axis=1).astype(BF16)

    pl.semaphore_wait(barrier, len(greeted))

    def send(src, dst, sems, first, device):
        return pltpu.make_async_remote_copy(
            src_ref=src,
            dst_ref=dst,
            send_sem=sems.at[first],
            recv_sem=sems.at[first + 1],
            device_id=device,
            device_id_type=MESH,
        )

    def drain(ref, sems, first):
        pltpu.make_async_copy(ref, ref, sems.at[first]).wait()
        pltpu.make_async_copy(ref, ref, sems.at[first + 1]).wait()

    for peer in span_peers:
        send(flow_own, flows.at[s], flow_sems, 0, (p, peer, q)).start()

    flows[s] = flow_own[...]

    lane = iota((8, 128), 1)
    source_lane = 127 * other
    near = lax.bitwise_and(lane + 128 - source_lane, 127)
    offset = pl.multiple_of(other * 128, 128)

    def pack(fields, tiles):
        parts = []
        for f in range(fields):
            for half in range(2):
                part = jnp.zeros((8, 128), F32)
                for i in range(cp):
                    spot = (f * 2 + half) * 16 + i
                    tile = tiles(f, i, half)
                    part = jnp.where(near == spot, pltpu.roll(tile, spot, 1) if spot else tile, part)
                parts.append(part)
        while len(parts) > 1:
            parts = [sum(parts[n : n + 2]) for n in range(0, len(parts), 2)]
        return jnp.where(q == 0, pltpu.roll(parts[0], 1, 1), parts[0])

    def halo(ref, step, count):
        pitch, span = pitch_sems.at[step], span_sems.at[step]
        return [
            send(ref.at[0:count, cp], ref.at[0:count, 0], pitch, 0, (up, s, q)),
            send(ref.at[0:count, 1], ref.at[0:count, cp + 1], pitch, 2, (down, s, q)),
            send(span_send.at[step, 0, 0:count], span_recv.at[step, 1, 0:count], span, 0, (p, inner, q)),
            send(span_send.at[step, 1, 0:count], span_recv.at[step, 0, 0:count], span, 2, (p, outer, q)),
        ]

    planes = (planes_first, planes_second)

    def swap_plane(step):
        return send(plane_send.at[step], plane_in.at[step], plane_sems.at[step], 0, (p, s, other))

    def spread_z(step):
        for peer in z_peers:
            send(plane_in.at[step], planes[step].at[x, z], plane_sems.at[step], 2, (peer, s, q)).start()
        planes[step][x, z] = plane_in[step]

    def spread_x(step):
        drain(planes[step].at[0, 0 : DEEP - 1], plane_sems.at[step], 2)
        for peer in x_peers:
            send(planes[step].at[x], planes[step].at[x], plane_sems.at[step], 4, (peer, s, q)).start()

    def wait_plane(step):
        drain(planes[step].at[0 : wide - 1], plane_sems.at[step], 4)

    loads[2].wait()
    loads[3].wait()
    plane_send[0] = pack(4, lambda f, i, half: state[f, i + 1, pl.ds(half * 8, 8), pl.ds(offset, 128)])

    swap = swap_plane(0)
    swap.start()
    first = halo(state, 0, 4)
    for copy in first[:2]:
        copy.start()

    @pl.loop(0, cp)
    def _(i):
        for f in range(4):
            span_send[0, 0, f, pl.ds(i, 1), :] = state[f, i + 1, 0:1, :]
            span_send[0, 1, f, pl.ds(i, 1), :] = state[f, i + 1, cr - 1 : cr, :]

    for copy in first[2:]:
        copy.start()

    for f in range(3):
        block = state[f, 1 : cp + 1].reshape(cp * cr, ca)
        high, low = halves(block)
        fparts[0, f] = high
        fparts[1, f] = low
    loads[1].wait()
    loads[4].wait()
    numbers = iota((256, CHUNK), 0).astype(F32).astype(BF16)
    one, zero = jnp.asarray(1, BF16), jnp.asarray(0, BF16)
    counts[...] = jnp.zeros((npitch, 1), F32)
    before = (iota((CHUNK, CHUNK), 0) < iota((CHUNK, CHUNK), 1)).astype(F32).astype(BF16)

    def sample(chunk):
        here = pl.ds(chunk * CHUNK, CHUNK)
        cell = cells[0:1, here]
        axial = lax.bitwise_and(cell, ca - 1)
        place = lax.shift_right_logical(cell, 8)
        onehot = jnp.where(numbers == axial.astype(F32).astype(BF16), one, zero)
        at_place = iota((cp * cr, CHUNK), 0) == place
        for f in range(3):
            picked = dot(fparts[0, f], onehot) + dot(fparts[1, f], onehot)
            sampled[f : f + 1, here] = jnp.sum(jnp.where(at_place, picked, 0.0), axis=0, keepdims=True)
        goal = dest[0:1, here]
        mine = iota((npitch, CHUNK), 0) == goal
        mine_f = mine.astype(F32)
        rank = dot(mine_f.astype(BF16), before) + counts[...]
        slots[0:1, here] = jnp.sum(jnp.where(mine, rank, 0.0), axis=0, keepdims=True)
        counts[...] += jnp.sum(mine_f, axis=1, keepdims=True)

    sample(0)
    swap.wait()
    spread_z(0)
    sample(1)
    spread_x(0)
    sample(2)

    some = flows.at[0 : nspan - 1]
    pltpu.make_async_copy(some, some, flow_sems.at[0]).wait()
    pltpu.make_async_copy(some, some, flow_sems.at[1]).wait()

    loads[5].wait()
    kernel_rows = radial[pl.ds(pl.multiple_of(s * cr, cr), cr), :]
    smoothed = dot(kernel_rows, flows[...].reshape(nspan * cr, 2 * ca))
    speed_axial = AXIAL_SPEED * (1.0 + 0.5 * jnp.tanh(smoothed[:, :ca]))
    speed_pitch = PITCH_SPEED * jnp.tanh(smoothed[:, ca:])
    speeds[0] = speed_axial
    speeds[1] = speed_pitch
    edge = jnp.where(q == 0, speed_axial[:, ca - 1 : ca], speed_axial[:, 0:1])
    speed_send[...] = jnp.broadcast_to(edge, (cr, 128))
    speed_copy = send(speed_send, speed_recv, speed_sems, 0, (p, s, other))
    speed_copy.start()
    sample(3)

    loads[6].wait()
    hand[...] = jnp.zeros(hand.shape, F32)
    speed_parts = halves(speeds[...].reshape(2 * cr, ca))

    def pass_on(chunk):
        here = pl.ds(chunk * CHUNK, CHUNK)
        cell = cells[0:1, here]
        axial = lax.bitwise_and(cell, ca - 1)
        onehot = jnp.where(numbers == axial.astype(F32).astype(BF16), one, zero)
        picked = dot(speed_parts[0], onehot) + dot(speed_parts[1], onehot)
        radius = lax.bitwise_and(lax.shift_right_logical(cell, 8), cr - 1)
        at_radius = iota((cr, CHUNK), 0) == radius
        got = [sampled[f : f + 1, here] for f in range(3)]
        for k in range(2):
            got.append(jnp.sum(jnp.where(at_radius, picked[k * cr : (k + 1) * cr], 0.0), axis=0, keepdims=True))
        which = iota((16, CHUNK), 0)
        item = jnp.where(which >= 5, which - 5, which)
        samples = jnp.zeros((16, CHUNK), F32)
        for k in range(5):
            samples = jnp.where(item == k, got[k], samples)
        old = jnp.concatenate([values[:, here], jnp.zeros((6, CHUNK), F32)], axis=0)
        updated = jnp.where(which < 5, old + 0.5 * (samples - old), old + 0.8 * samples)
        high, low = halves(updated)
        goal = dest[0:1, here]
        odd = lax.bitwise_and(goal, 1).astype(F32)
        column = (slots[0:1, here] + 128.0 * odd).astype(BF16)
        hot = jnp.where(numbers == column, one, zero)
        pair = jnp.broadcast_to(lax.shift_right_logical(goal, 1).astype(F32), (16, CHUNK)).astype(BF16)
        pair = jnp.concatenate([pair, pair], axis=1)
        both = jnp.concatenate([high, low], axis=1)
        left = jnp.concatenate([jnp.where(pair == jnp.asarray(d, BF16), both, zero) for d in range(npitch // 2)], axis=0)
        hand[...] += dot_nt(left, jnp.concatenate([hot, hot], axis=1))

    for chunk in range(nchunk):
        pass_on(chunk)
    for d in range(npitch):
        row, column = d // 2 * 16, d % 2 * 128
        outgoing[d % DEEP, d // DEEP] = hand[row : row + 10, column : column + 128]
    for step, peer in enumerate(z_peers):
        far = wrap(z + step + 1, DEEP)
        send(outgoing.at[far], midway.at[z], hand_sems, 0, (peer, s, q)).start()
    midway[z] = outgoing[z]

    wait_plane(0)
    for copy in first:
        copy.wait()
    speed_copy.wait()

    start_cell = map_ref[0, 0]
    facing = lax.shift_right_logical(start_cell, 4)
    shift = lax.bitwise_and(start_cell, 15)
    facing_next = lax.bitwise_and(facing + 1, npitch - 1)
    in_group = lax.bitwise_and(lane, 15)

    def ghost(step, count):
        low = planes[step][lax.shift_right_logical(facing, 3), lax.bitwise_and(facing, DEEP - 1)]
        high = planes[step][lax.shift_right_logical(facing_next, 3), lax.bitwise_and(facing_next, DEEP - 1)]
        high = pltpu.roll(high, 16, 1)
        for bit in range(4):
            moved = lax.bitwise_and(shift, 1 << bit) != 0
            low = jnp.where(moved, pltpu.roll(low, 128 - (1 << bit), 1), low)
            high = jnp.where(moved, pltpu.roll(high, 128 - (1 << bit), 1), high)
        window = jnp.where(in_group + shift < 16, low, high)

        for f in range(count):
            for half in range(2):
                for i in range(cp):
                    spot = (f * 2 + half) * 16 + i
                    ghosts[f, i, half * 8 : half * 8 + 8, :] = jnp.broadcast_to(window[:, spot : spot + 1], (8, 128))

    ghost(0, 4)
    lanes = iota((cr, ca), 1)
    radii = iota((cr, ca), 0)
    west, east = lanes == 0, lanes == ca - 1
    hub, tip = radii == 0, radii == cr - 1
    stator = q == 0
    span_first = s == 0
    span_last = s == nspan - 1

    def twice(x):
        return jnp.concatenate([x, x], axis=1)

    def around(x, inner_row, outer_row, ghost_tile):
        out = jnp.where(tip, outer_row, pltpu.roll(x, cr - 1, 0))
        inn = jnp.where(hub, inner_row, pltpu.roll(x, 1, 0))
        right = jnp.where(east, ghost_tile, pltpu.roll(x, ca - 1, 1))
        left = jnp.where(west, ghost_tile, pltpu.roll(x, 1, 1))
        return out, inn, right, left

    sa = speeds[0]
    sp = speeds[1]
    ghost_speed = twice(speed_recv[...])
    no_west = jnp.logical_and(west, stator)
    no_east = jnp.logical_and(east, jnp.logical_not(stator))
    sa_right = jnp.where(no_east, sa, jnp.where(east, ghost_speed, pltpu.roll(sa, ca - 1, 1)))
    sa_left = jnp.where(no_west, sa, jnp.where(west, ghost_speed, pltpu.roll(sa, 1, 1)))
    w_east = 0.5 * (sa + sa_right)
    w_west = 0.5 * (sa + sa_left)
    ep, em = jnp.maximum(w_east, 0.0), jnp.minimum(w_east, 0.0)
    wp, wm = jnp.maximum(w_west, 0.0), jnp.minimum(w_west, 0.0)
    pp, pm = jnp.maximum(sp, 0.0), jnp.minimum(sp, 0.0)
    no_inner = jnp.logical_and(hub, span_first)
    no_outer = jnp.logical_and(tip, span_last)

    @pl.loop(0, cp, unroll=UNROLL)
    def _(i):
        k = state[3, i + 1]
        k_out, k_in, k_right, k_left = around(
            k, span_recv[0, 0, 3, pl.ds(i, 1), :], span_recv[0, 1, 3, pl.ds(i, 1), :], twice(ghosts[3, i])
        )
        k_right = jnp.where(no_east, k, k_right)
        k_left = jnp.where(no_west, k, k_left)
        d_up = 0.5 * (k + state[3, i + 2])
        d_down = 0.5 * (k + state[3, i])
        d_out = jnp.where(no_outer, 0.0, 0.5 * (k + k_out))
        d_in = jnp.where(no_inner, 0.0, 0.5 * (k + k_in))
        d_east = 0.5 * (k + k_right)
        d_west = 0.5 * (k + k_left)
        c_up = TIME_STEP * (d_up - pm)
        c_down = TIME_STEP * (d_down + pp)
        c_out = TIME_STEP * d_out
        c_in = TIME_STEP * d_in
        c_east = TIME_STEP * (d_east - em)
        c_west = TIME_STEP * (d_west + wp)
        center = 1.0 - (c_up + c_down + c_out + c_in) - TIME_STEP * (ep + d_east + d_west - wm)
        center = center + jnp.where(no_east, c_east, 0.0) + jnp.where(no_west, c_west, 0.0)
        coef[0, i] = center
        coef[1, i] = c_up
        coef[2, i] = c_down
        coef[3, i] = c_out
        coef[4, i] = c_in
        coef[5, i] = jnp.where(no_east, 0.0, c_east)
        coef[6, i] = jnp.where(no_west, 0.0, c_west)

    def advance(old, step, store):
        @pl.loop(0, cp, unroll=UNROLL)
        def _(i):
            c = [coef[n, i] for n in range(7)]
            for f in range(3):
                v = old[f, i + 1]
                out, inn, right, left = around(
                    v, span_recv[step, 0, f, pl.ds(i, 1), :], span_recv[step, 1, f, pl.ds(i, 1), :], twice(ghosts[f, i])
                )
                new = c[0] * v + c[1] * old[f, i + 2] + c[2] * old[f, i]
                new = new + c[3] * out + c[4] * inn + c[5] * right + c[6] * left
                store(f, i, new)

    def store_first(f, i, new):
        state2[f, i + 1] = new
        span_send[1, 0, f, pl.ds(i, 1), :] = new[0:1, :]
        span_send[1, 1, f, pl.ds(i, 1), :] = new[cr - 1 : cr, :]

    advance(state, 0, store_first)

    second = halo(state2, 1, 3)
    for copy in second:
        copy.start()
    plane_send[1] = pack(3, lambda f, i, half: state2[f, i + 1, pl.ds(half * 8, 8), pl.ds(offset, 128)])
    swap = swap_plane(1)
    swap.start()

    swap.wait()
    spread_z(1)
    drain(midway.at[0 : DEEP - 1], hand_sems, 0)
    for step, peer in enumerate(x_peers):
        far = wrap(x + step + 1, wide)
        send(midway.at[:, far], landed.at[x], hand_sems, 2, (peer, s, q)).start()
    landed[x] = midway[:, x]
    spread_x(1)
    for copy in second:
        copy.wait()
    wait_plane(1)
    ghost(1, 3)

    def store_second(f, i, new):
        advected_ref[f, i] = new

    advance(state2, 1, store_second)

    drain(landed.at[0 : wide - 1], hand_sems, 2)
    for d in range(npitch):
        arrived_ref[:, d * 128 : (d + 1) * 128] = landed[d // DEEP, d % DEEP]


def local(fields, diffusivity, mean_flow, radial_kernel, tracer_values, tracer_cells, tracer_dest, interface_map):
    npitch = lax.axis_size("pitch")
    nspan = lax.axis_size("span")
    tracers = tracer_values.shape[1]
    anywhere = pl.BlockSpec(memory_space=pltpu.HBM)
    vmem = pl.BlockSpec(memory_space=pltpu.VMEM)
    dma = pltpu.SemaphoreType.DMA
    return pl.pallas_call(
        functools.partial(kernel, npitch, nspan),
        out_shape=(
            pltpu.VMEM((3, 16, 16, 256), F32),
            pltpu.VMEM((10, npitch * 128), F32),
        ),
        in_specs=[anywhere] * 7 + [pl.BlockSpec(memory_space=pltpu.SMEM)],
        out_specs=(vmem, vmem),
        scratch_shapes=[
            pltpu.VMEM((4, 18, 16, 256), F32),
            pltpu.VMEM((16, 2, 256), BF16),
            pltpu.VMEM((128, nspan * 16), BF16),
            pltpu.VMEM((10, tracers), F32),
            pltpu.VMEM((1, tracers), jnp.int32),
            pltpu.VMEM((1, tracers), jnp.int32),
            pltpu.VMEM((16, 512), BF16),
            pltpu.VMEM((nspan, 16, 512), BF16),
            pltpu.VMEM((3, 18, 16, 256), F32),
            pltpu.VMEM((2, 2, 4, 16, 256), F32),
            pltpu.VMEM((2, 2, 4, 16, 256), F32),
            pltpu.VMEM((2, 8, 128), F32),
            pltpu.VMEM((2, 8, 128), F32),
            pltpu.VMEM((npitch // DEEP, DEEP, 8, 128), F32),
            pltpu.VMEM((npitch // DEEP, DEEP, 8, 128), F32),
            pltpu.VMEM((16, 128), F32),
            pltpu.VMEM((16, 128), F32),
            pltpu.VMEM((DEEP, npitch // DEEP, 10, 128), F32),
            pltpu.VMEM((DEEP, npitch // DEEP, 10, 128), F32),
            pltpu.VMEM((npitch // DEEP, DEEP, 10, 128), F32),
            pltpu.VMEM((2, 3, 256, 256), BF16),
            pltpu.VMEM((8, tracers), F32),
            pltpu.VMEM((8, tracers), F32),
            pltpu.VMEM((npitch, 1), F32),
            pltpu.VMEM((npitch * 8, 256), F32),
            pltpu.VMEM((2, 16, 256), F32),
            pltpu.VMEM((7, 16, 16, 256), F32),
            pltpu.VMEM((4, 16, 16, 128), F32),
            dma((7,)),
            dma((2,)),
            dma((2, 4)),
            dma((2, 4)),
            dma((2, 6)),
            dma((2,)),
            dma((4,)),
        ],
        compiler_params=pltpu.CompilerParams(
            collective_id=0, has_side_effects=True, vmem_limit_bytes=60 * 1024 * 1024
        ),
        name="row_step",
    )(
        fields,
        diffusivity,
        mean_flow,
        radial_kernel,
        tracer_values,
        tracer_cells.reshape(1, tracers),
        tracer_dest.reshape(1, tracers),
        interface_map,
    )


def solution(mesh):
    placed = (
        P(None, "pitch", "span", "row"),
        P("pitch", "span", "row"),
        P("span", None, "row"),
        P(),
        P(None, ("pitch", "span", "row")),
        P(("pitch", "span", "row")),
        P(("pitch", "span", "row"), None),
        P("row", "pitch"),
    )
    return jax.shard_map(
        local,
        mesh=mesh,
        in_specs=placed,
        out_specs=(P(None, "pitch", "span", "row"), P(None, ("pitch", "span", "row"))),
        check_vma=False,
    )
```

```python
import functools

import jax
import jax.numpy as jnp
from jax import lax
from jax.experimental import pallas as pl
from jax.experimental.pallas import tpu as pltpu
from jax.sharding import PartitionSpec as P

TIME_STEP = 0.9
AXIAL_SPEED = 0.15
PITCH_SPEED = 0.15
CHUNK = 512
UNROLL = 16
DEEP = 8
MESH = pl.DeviceIdType.MESH
F32 = jnp.float32
BF16 = jnp.bfloat16


def iota(shape, dim):
    return lax.broadcasted_iota(jnp.int32, shape, dim)


def halves(x):
    high = x.astype(BF16)
    return high, (x - high.astype(F32)).astype(BF16)


def dot(a, b):
    return jnp.dot(a, b, preferred_element_type=F32)


def dot_nt(a, b):
    return lax.dot_general(a, b, (((1,), (1,)), ((), ())), preferred_element_type=F32)


def kernel(
    npitch,
    nspan,
    fields_hbm,
    kappa_hbm,
    flow_hbm,
    radial_hbm,
    values_hbm,
    cells_hbm,
    dest_hbm,
    map_ref,
    advected_ref,
    arrived_ref,
    state,
    flow_raw,
    radial,
    values,
    cells,
    dest,
    flow_own,
    flows,
    state2,
    span_send,
    span_recv,
    plane_send,
    planes_first,
    planes_second,
    speed_send,
    speed_recv,
    outgoing,
    midway,
    landed,
    fparts,
    sampled,
    slots,
    counts,
    hand,
    speeds,
    coef,
    load_sem,
    flow_sems,
    pitch_sems,
    span_sems,
    plane_sems,
    speed_sems,
    hand_sems,
):
    p = lax.axis_index("pitch")
    s = lax.axis_index("span")
    q = lax.axis_index("row")
    other = 1 - q
    cp, cr, ca = 16, 16, 256
    tracers = values.shape[1]
    nchunk = tracers // CHUNK

    loads = [
        pltpu.make_async_copy(flow_hbm, flow_raw, load_sem.at[0]),
        pltpu.make_async_copy(dest_hbm, dest, load_sem.at[1]),
        pltpu.make_async_copy(fields_hbm, state.at[0:3, 1 : cp + 1], load_sem.at[2]),
        pltpu.make_async_copy(kappa_hbm, state.at[3, 1 : cp + 1], load_sem.at[3]),
        pltpu.make_async_copy(cells_hbm, cells, load_sem.at[4]),
        pltpu.make_async_copy(radial_hbm, radial, load_sem.at[5]),
        pltpu.make_async_copy(values_hbm, values, load_sem.at[6]),
    ]
    for copy in loads:
        copy.start()

    def wrap(index, count):
        return lax.bitwise_and(index, count - 1)

    barrier = pltpu.get_barrier_semaphore()

    wide = npitch // DEEP
    x, z = lax.shift_right_logical(p, 3), lax.bitwise_and(p, DEEP - 1)
    z_peers = [x * DEEP + wrap(z + step, DEEP) for step in range(1, DEEP)]
    x_peers = [wrap(p + step * DEEP, npitch) for step in range(1, wide)]
    span_peers = [wrap(s + step, nspan) for step in range(1, nspan)]
    up, down = wrap(p + 1, npitch), wrap(p + npitch - 1, npitch)
    outer, inner = wrap(s + 1, nspan), wrap(s + nspan - 1, nspan)
    greeted = [(up, s, q), (down, s, q)]
    greeted += [(p, peer, q) for peer in span_peers]
    greeted += [(peer, s, other) for peer in [p] + z_peers]
    greeted += [(peer, s, q) for peer in z_peers + x_peers]
    for device in greeted:
        pl.semaphore_signal(barrier, inc=1, device_id=device, device_id_type=MESH)

    loads[0].wait()
    raw = flow_raw[...].astype(F32)
    flow_own[...] = jnp.concatenate([raw[:, 0, :], raw[:, 1, :]], axis=1).astype(BF16)

    pl.semaphore_wait(barrier, len(greeted))

    def send(src, dst, sems, first, device):
        return pltpu.make_async_remote_copy(
            src_ref=src,
            dst_ref=dst,
            send_sem=sems.at[first],
            recv_sem=sems.at[first + 1],
            device_id=device,
            device_id_type=MESH,
        )

    def drain(ref, sems, first):
        pltpu.make_async_copy(ref, ref, sems.at[first]).wait()
        pltpu.make_async_copy(ref, ref, sems.at[first + 1]).wait()

    for peer in span_peers:
        send(flow_own, flows.at[s], flow_sems, 0, (p, peer, q)).start()

    flows[s] = flow_own[...]

    lane = iota((8, 128), 1)
    source_lane = 127 * other
    near = lax.bitwise_and(lane + 128 - source_lane, 127)
    offset = pl.multiple_of(other * 128, 128)

    def pack(fields, tiles):
        parts = []
        for f in range(fields):
            for half in range(2):
                part = jnp.zeros((8, 128), F32)
                for i in range(cp):
                    spot = (f * 2 + half) * 16 + i
                    tile = tiles(f, i, half)
                    part = jnp.where(near == spot, pltpu.roll(tile, spot, 1) if spot else tile, part)
                parts.append(part)
        while len(parts) > 1:
            parts = [sum(parts[n : n + 2]) for n in range(0, len(parts), 2)]
        return jnp.where(q == 0, pltpu.roll(parts[0], 1, 1), parts[0])

    def halo(ref, step, count):
        pitch, span = pitch_sems.at[step], span_sems.at[step]
        return [
            send(ref.at[0:count, cp], ref.at[0:count, 0], pitch, 0, (up, s, q)),
            send(ref.at[0:count, 1], ref.at[0:count, cp + 1], pitch, 2, (down, s, q)),
            send(span_send.at[step, 0, 0:count], span_recv.at[step, 1, 0:count], span, 0, (p, inner, q)),
            send(span_send.at[step, 1, 0:count], span_recv.at[step, 0, 0:count], span, 2, (p, outer, q)),
        ]

    planes = (planes_first, planes_second)

    def spread_z(step):
        for peer in [p] + z_peers:
            send(plane_send.at[step], planes[step].at[x, z], plane_sems.at[step], 0, (peer, s, other)).start()

    def spread_x(step):
        drain(planes[step].at[0], plane_sems.at[step], 0)
        for peer in x_peers:
            send(planes[step].at[x], planes[step].at[x], plane_sems.at[step], 2, (peer, s, q)).start()

    def wait_plane(step):
        drain(planes[step].at[0 : wide - 1], plane_sems.at[step], 2)

    loads[2].wait()
    loads[3].wait()
    plane_send[0] = pack(4, lambda f, i, half: state[f, i + 1, pl.ds(half * 8, 8), pl.ds(offset, 128)])

    spread_z(0)
    first = halo(state, 0, 4)
    for copy in first[:2]:
        copy.start()

    @pl.loop(0, cp)
    def _(i):
        for f in range(4):
            span_send[0, 0, f, pl.ds(i, 1), :] = state[f, i + 1, 0:1, :]
            span_send[0, 1, f, pl.ds(i, 1), :] = state[f, i + 1, cr - 1 : cr, :]

    for copy in first[2:]:
        copy.start()

    for f in range(3):
        block = state[f, 1 : cp + 1].reshape(cp * cr, ca)
        high, low = halves(block)
        fparts[0, f] = high
        fparts[1, f] = low
    loads[1].wait()
    loads[4].wait()
    numbers = iota((256, CHUNK), 0).astype(F32).astype(BF16)
    one, zero = jnp.asarray(1, BF16), jnp.asarray(0, BF16)
    counts[...] = jnp.zeros((npitch, 1), F32)
    before = (iota((CHUNK, CHUNK), 0) < iota((CHUNK, CHUNK), 1)).astype(F32).astype(BF16)

    def sample(chunk):
        here = pl.ds(chunk * CHUNK, CHUNK)
        cell = cells[0:1, here]
        axial = lax.bitwise_and(cell, ca - 1)
        place = lax.shift_right_logical(cell, 8)
        onehot = jnp.where(numbers == axial.astype(F32).astype(BF16), one, zero)
        at_place = iota((cp * cr, CHUNK), 0) == place
        for f in range(3):
            picked = dot(fparts[0, f], onehot) + dot(fparts[1, f], onehot)
            sampled[f : f + 1, here] = jnp.sum(jnp.where(at_place, picked, 0.0), axis=0, keepdims=True)
        goal = dest[0:1, here]
        mine = iota((npitch, CHUNK), 0) == goal
        mine_f = mine.astype(F32)
        rank = dot(mine_f.astype(BF16), before) + counts[...]
        slots[0:1, here] = jnp.sum(jnp.where(mine, rank, 0.0), axis=0, keepdims=True)
        counts[...] += jnp.sum(mine_f, axis=1, keepdims=True)

    sample(0)
    sample(1)
    spread_x(0)
    sample(2)

    some = flows.at[0 : nspan - 1]
    pltpu.make_async_copy(some, some, flow_sems.at[0]).wait()
    pltpu.make_async_copy(some, some, flow_sems.at[1]).wait()

    loads[5].wait()
    kernel_rows = radial[pl.ds(pl.multiple_of(s * cr, cr), cr), :]
    smoothed = dot(kernel_rows, flows[...].reshape(nspan * cr, 2 * ca))
    speed_axial = AXIAL_SPEED * (1.0 + 0.5 * jnp.tanh(smoothed[:, :ca]))
    speed_pitch = PITCH_SPEED * jnp.tanh(smoothed[:, ca:])
    speeds[0] = speed_axial
    speeds[1] = speed_pitch
    edge = jnp.where(q == 0, speed_axial[:, ca - 1 : ca], speed_axial[:, 0:1])
    speed_send[...] = jnp.broadcast_to(edge, (cr, 128))
    speed_copy = send(speed_send, speed_recv, speed_sems, 0, (p, s, other))
    speed_copy.start()
    sample(3)

    loads[6].wait()
    hand[...] = jnp.zeros(hand.shape, F32)
    speed_parts = halves(speeds[...].reshape(2 * cr, ca))

    def pass_on(chunk):
        here = pl.ds(chunk * CHUNK, CHUNK)
        cell = cells[0:1, here]
        axial = lax.bitwise_and(cell, ca - 1)
        onehot = jnp.where(numbers == axial.astype(F32).astype(BF16), one, zero)
        picked = dot(speed_parts[0], onehot) + dot(speed_parts[1], onehot)
        radius = lax.bitwise_and(lax.shift_right_logical(cell, 8), cr - 1)
        at_radius = iota((cr, CHUNK), 0) == radius
        got = [sampled[f : f + 1, here] for f in range(3)]
        for k in range(2):
            got.append(jnp.sum(jnp.where(at_radius, picked[k * cr : (k + 1) * cr], 0.0), axis=0, keepdims=True))
        which = iota((16, CHUNK), 0)
        item = jnp.where(which >= 5, which - 5, which)
        samples = jnp.zeros((16, CHUNK), F32)
        for k in range(5):
            samples = jnp.where(item == k, got[k], samples)
        old = jnp.concatenate([values[:, here], jnp.zeros((6, CHUNK), F32)], axis=0)
        updated = jnp.where(which < 5, old + 0.5 * (samples - old), old + 0.8 * samples)
        high, low = halves(updated)
        goal = dest[0:1, here]
        odd = lax.bitwise_and(goal, 1).astype(F32)
        column = (slots[0:1, here] + 128.0 * odd).astype(BF16)
        hot = jnp.where(numbers == column, one, zero)
        pair = jnp.broadcast_to(lax.shift_right_logical(goal, 1).astype(F32), (16, CHUNK)).astype(BF16)
        pair = jnp.concatenate([pair, pair], axis=1)
        both = jnp.concatenate([high, low], axis=1)
        left = jnp.concatenate([jnp.where(pair == jnp.asarray(d, BF16), both, zero) for d in range(npitch // 2)], axis=0)
        hand[...] += dot_nt(left, jnp.concatenate([hot, hot], axis=1))

    for chunk in range(nchunk):
        pass_on(chunk)
    for d in range(npitch):
        row, column = d // 2 * 16, d % 2 * 128
        outgoing[d % DEEP, d // DEEP] = hand[row : row + 10, column : column + 128]
    for step, peer in enumerate(z_peers):
        far = wrap(z + step + 1, DEEP)
        send(outgoing.at[far], midway.at[z], hand_sems, 0, (peer, s, q)).start()
    midway[z] = outgoing[z]

    for copy in first:
        copy.wait()

    start_cell = map_ref[0, 0]
    facing = lax.shift_right_logical(start_cell, 4)
    shift = lax.bitwise_and(start_cell, 15)
    facing_next = lax.bitwise_and(facing + 1, npitch - 1)
    in_group = lax.bitwise_and(lane, 15)

    def facing_plane(step):
        low = planes[step][lax.shift_right_logical(facing, 3), lax.bitwise_and(facing, DEEP - 1)]
        high = planes[step][lax.shift_right_logical(facing_next, 3), lax.bitwise_and(facing_next, DEEP - 1)]
        high = pltpu.roll(high, 16, 1)
        for bit in range(4):
            moved = lax.bitwise_and(shift, 1 << bit) != 0
            low = jnp.where(moved, pltpu.roll(low, 128 - (1 << bit), 1), low)
            high = jnp.where(moved, pltpu.roll(high, 128 - (1 << bit), 1), high)
        return jnp.where(in_group + shift < 16, low, high)

    def add_to_plane(ref, first_cell, delta):
        for f in range(3):
            for half in range(2):
                for i in range(cp):
                    spot = (f * 2 + half) * 16 + i
                    where = (f, i + first_cell, pl.ds(half * 8, 8), pl.ds(offset, 128))
                    term = jnp.broadcast_to(delta[:, spot : spot + 1], (8, 128))
                    ref[where] += jnp.where(near == 0, term, 0.0)

    lanes = iota((cr, ca), 1)
    radii = iota((cr, ca), 0)
    west, east = lanes == 0, lanes == ca - 1
    hub, tip = radii == 0, radii == cr - 1
    stator = q == 0
    span_first = s == 0
    span_last = s == nspan - 1

    def around(x, inner_row, outer_row):
        out = jnp.where(tip, outer_row, pltpu.roll(x, cr - 1, 0))
        inn = jnp.where(hub, inner_row, pltpu.roll(x, 1, 0))
        right = pltpu.roll(x, ca - 1, 1)
        left = pltpu.roll(x, 1, 1)
        return out, inn, right, left

    sa = speeds[0]
    sp = speeds[1]
    no_west = jnp.logical_and(west, stator)
    no_east = jnp.logical_and(east, jnp.logical_not(stator))
    east_open = jnp.where(jnp.logical_and(east, stator), 0.0, 1.0)
    west_open = jnp.where(jnp.logical_and(west, jnp.logical_not(stator)), 0.0, 1.0)
    sa_right = jnp.where(no_east, sa, pltpu.roll(sa, ca - 1, 1))
    sa_left = jnp.where(no_west, sa, pltpu.roll(sa, 1, 1))
    w_east = 0.5 * (sa + sa_right) * east_open
    w_west = 0.5 * (sa + sa_left) * west_open
    ep, em = jnp.maximum(w_east, 0.0), jnp.minimum(w_east, 0.0)
    wp, wm = jnp.maximum(w_west, 0.0), jnp.minimum(w_west, 0.0)
    pp, pm = jnp.maximum(sp, 0.0), jnp.minimum(sp, 0.0)
    no_inner = jnp.logical_and(hub, span_first)
    no_outer = jnp.logical_and(tip, span_last)

    @pl.loop(0, cp, unroll=UNROLL)
    def _(i):
        k = state[3, i + 1]
        k_out, k_in, k_right, k_left = around(
            k, span_recv[0, 0, 3, pl.ds(i, 1), :], span_recv[0, 1, 3, pl.ds(i, 1), :]
        )
        k_right = jnp.where(no_east, k, k_right)
        k_left = jnp.where(no_west, k, k_left)
        d_up = 0.5 * (k + state[3, i + 2])
        d_down = 0.5 * (k + state[3, i])
        d_out = jnp.where(no_outer, 0.0, 0.5 * (k + k_out))
        d_in = jnp.where(no_inner, 0.0, 0.5 * (k + k_in))
        d_east = 0.5 * (k + k_right) * east_open
        d_west = 0.5 * (k + k_left) * west_open
        c_up = TIME_STEP * (d_up - pm)
        c_down = TIME_STEP * (d_down + pp)
        c_out = TIME_STEP * d_out
        c_in = TIME_STEP * d_in
        c_east = TIME_STEP * (d_east - em)
        c_west = TIME_STEP * (d_west + wp)
        center = 1.0 - (c_up + c_down + c_out + c_in) - TIME_STEP * (ep + d_east + d_west - wm)
        center = center + jnp.where(no_east, c_east, 0.0) + jnp.where(no_west, c_west, 0.0)
        coef[0, i] = center
        coef[1, i] = c_up
        coef[2, i] = c_down
        coef[3, i] = c_out
        coef[4, i] = c_in
        coef[5, i] = jnp.where(no_east, 0.0, c_east)
        coef[6, i] = jnp.where(no_west, 0.0, c_west)

    def advance(old, step, store):
        @pl.loop(0, cp, unroll=UNROLL)
        def _(i):
            c = [coef[n, i] for n in range(7)]
            for f in range(3):
                v = old[f, i + 1]
                out, inn, right, left = around(
                    v, span_recv[step, 0, f, pl.ds(i, 1), :], span_recv[step, 1, f, pl.ds(i, 1), :]
                )
                new = c[0] * v + c[1] * old[f, i + 2] + c[2] * old[f, i]
                new = new + c[3] * out + c[4] * inn + c[5] * right + c[6] * left
                store(f, i, new)

    def store_first(f, i, new):
        state2[f, i + 1] = new

    advance(state, 0, store_first)

    base = pack(3, lambda f, i, half: state2[f, i + 1, pl.ds(half * 8, 8), pl.ds(offset, 128)])
    plane_send[1] = base
    spread_z(1)

    wait_plane(0)
    speed_copy.wait()
    own = plane_send[0]
    facing_own = facing_plane(0)
    k_sum = 0.5 * (own + facing_own)
    field = lax.shift_right_logical(lane, 5)
    k_face = jnp.where(field == 0, pltpu.roll(k_sum, 32, 1), k_sum)
    k_face = jnp.where(field == 1, pltpu.roll(k_sum, 64, 1), k_face)
    k_face = jnp.where(field == 2, pltpu.roll(k_sum, 96, 1), k_face)
    speed_sum = 0.5 * (speed_send[...] + speed_recv[...])
    w_face = jnp.where(lax.bitwise_and(lane, 16) == 0, speed_sum[0:8], speed_sum[8:16])
    w_plus, w_minus = jnp.maximum(w_face, 0.0), jnp.minimum(w_face, 0.0)
    sign = jnp.where(q == 0, -TIME_STEP, TIME_STEP)

    def change(mine, theirs):
        lower = jnp.where(q == 0, mine, theirs)
        upper = jnp.where(q == 0, theirs, mine)
        return sign * (w_plus * lower + w_minus * upper - k_face * (upper - lower))

    delta = change(own, facing_own)
    add_to_plane(state2, 1, delta)

    @pl.loop(0, cp)
    def _(i):
        for f in range(3):
            span_send[1, 0, f, pl.ds(i, 1), :] = state2[f, i + 1, 0:1, :]
            span_send[1, 1, f, pl.ds(i, 1), :] = state2[f, i + 1, cr - 1 : cr, :]

    second = halo(state2, 1, 3)
    for copy in second:
        copy.start()

    drain(midway.at[0 : DEEP - 1], hand_sems, 0)
    for step, peer in enumerate(x_peers):
        far = wrap(x + step + 1, wide)
        send(midway.at[:, far], landed.at[x], hand_sems, 2, (peer, s, q)).start()
    spread_x(1)
    landed[x] = midway[:, x]
    for copy in second:
        copy.wait()

    def store_second(f, i, new):
        advected_ref[f, i] = new

    advance(state2, 1, store_second)
    wait_plane(1)
    add_to_plane(advected_ref, 0, change(base + delta, facing_plane(1) - delta))

    drain(landed.at[0 : wide - 1], hand_sems, 2)
    for d in range(npitch):
        arrived_ref[:, d * 128 : (d + 1) * 128] = landed[d // DEEP, d % DEEP]


def local(fields, diffusivity, mean_flow, radial_kernel, tracer_values, tracer_cells, tracer_dest, interface_map):
    npitch = lax.axis_size("pitch")
    nspan = lax.axis_size("span")
    tracers = tracer_values.shape[1]
    anywhere = pl.BlockSpec(memory_space=pltpu.HBM)
    vmem = pl.BlockSpec(memory_space=pltpu.VMEM)
    dma = pltpu.SemaphoreType.DMA
    return pl.pallas_call(
        functools.partial(kernel, npitch, nspan),
        out_shape=(
            pltpu.VMEM((3, 16, 16, 256), F32),
            pltpu.VMEM((10, npitch * 128), F32),
        ),
        in_specs=[anywhere] * 7 + [pl.BlockSpec(memory_space=pltpu.SMEM)],
        out_specs=(vmem, vmem),
        scratch_shapes=[
            pltpu.VMEM((4, 18, 16, 256), F32),
            pltpu.VMEM((16, 2, 256), BF16),
            pltpu.VMEM((128, nspan * 16), BF16),
            pltpu.VMEM((10, tracers), F32),
            pltpu.VMEM((1, tracers), jnp.int32),
            pltpu.VMEM((1, tracers), jnp.int32),
            pltpu.VMEM((16, 512), BF16),
            pltpu.VMEM((nspan, 16, 512), BF16),
            pltpu.VMEM((3, 18, 16, 256), F32),
            pltpu.VMEM((2, 2, 4, 16, 256), F32),
            pltpu.VMEM((2, 2, 4, 16, 256), F32),
            pltpu.VMEM((2, 8, 128), F32),
            pltpu.VMEM((npitch // DEEP, DEEP, 8, 128), F32),
            pltpu.VMEM((npitch // DEEP, DEEP, 8, 128), F32),
            pltpu.VMEM((16, 128), F32),
            pltpu.VMEM((16, 128), F32),
            pltpu.VMEM((DEEP, npitch // DEEP, 10, 128), F32),
            pltpu.VMEM((DEEP, npitch // DEEP, 10, 128), F32),
            pltpu.VMEM((npitch // DEEP, DEEP, 10, 128), F32),
            pltpu.VMEM((2, 3, 256, 256), BF16),
            pltpu.VMEM((8, tracers), F32),
            pltpu.VMEM((8, tracers), F32),
            pltpu.VMEM((npitch, 1), F32),
            pltpu.VMEM((npitch * 8, 256), F32),
            pltpu.VMEM((2, 16, 256), F32),
            pltpu.VMEM((7, 16, 16, 256), F32),
            dma((7,)),
            dma((2,)),
            dma((2, 4)),
            dma((2, 4)),
            dma((2, 4)),
            dma((2,)),
            dma((4,)),
        ],
        compiler_params=pltpu.CompilerParams(
            collective_id=0, has_side_effects=True, vmem_limit_bytes=60 * 1024 * 1024
        ),
        name="row_step",
    )(
        fields,
        diffusivity,
        mean_flow,
        radial_kernel,
        tracer_values,
        tracer_cells.reshape(1, tracers),
        tracer_dest.reshape(1, tracers),
        interface_map,
    )


def solution(mesh):
    placed = (
        P(None, "pitch", "span", "row"),
        P("pitch", "span", "row"),
        P("span", None, "row"),
        P(),
        P(None, ("pitch", "span", "row")),
        P(("pitch", "span", "row")),
        P(("pitch", "span", "row"), None),
        P("row", "pitch"),
    )
    return jax.shard_map(
        local,
        mesh=mesh,
        in_specs=placed,
        out_specs=(P(None, "pitch", "span", "row"), P(None, ("pitch", "span", "row"))),
        check_vma=False,
    )
```

```python
import functools

import jax
import jax.numpy as jnp
from jax import lax
from jax.experimental import pallas as pl
from jax.experimental.pallas import tpu as pltpu
from jax.sharding import PartitionSpec as P

TIME_STEP = 0.9
AXIAL_SPEED = 0.15
PITCH_SPEED = 0.15
CHUNK = 512
UNROLL = 16
DEEP = 8
MESH = pl.DeviceIdType.MESH
F32 = jnp.float32
BF16 = jnp.bfloat16


def iota(shape, dim):
    return lax.broadcasted_iota(jnp.int32, shape, dim)


def halves(x):
    high = x.astype(BF16)
    return high, (x - high.astype(F32)).astype(BF16)


def dot(a, b):
    return jnp.dot(a, b, preferred_element_type=F32)


def dot_nt(a, b):
    return lax.dot_general(a, b, (((1,), (1,)), ((), ())), preferred_element_type=F32)


def kernel(
    npitch,
    nspan,
    fields_hbm,
    kappa_hbm,
    flow_hbm,
    radial_hbm,
    values_hbm,
    cells_hbm,
    dest_hbm,
    map_ref,
    advected_ref,
    arrived_ref,
    state,
    flow_raw,
    radial,
    values,
    cells,
    dest,
    flow_own,
    flows,
    state2,
    span_send,
    span_recv,
    plane_send,
    planes_first,
    planes_second,
    speed_send,
    speed_recv,
    outgoing,
    landed,
    fparts,
    sampled,
    slots,
    counts,
    hand,
    speeds,
    coef,
    load_sem,
    flow_sems,
    pitch_sems,
    span_sems,
    plane_sems,
    speed_sems,
    hand_sems,
):
    p = lax.axis_index("pitch")
    s = lax.axis_index("span")
    q = lax.axis_index("row")
    other = 1 - q
    cp, cr, ca = 16, 16, 256
    tracers = values.shape[1]
    nchunk = tracers // CHUNK

    loads = [
        pltpu.make_async_copy(flow_hbm, flow_raw, load_sem.at[0]),
        pltpu.make_async_copy(dest_hbm, dest, load_sem.at[1]),
        pltpu.make_async_copy(fields_hbm, state.at[0:3, 1 : cp + 1], load_sem.at[2]),
        pltpu.make_async_copy(kappa_hbm, state.at[3, 1 : cp + 1], load_sem.at[3]),
        pltpu.make_async_copy(cells_hbm, cells, load_sem.at[4]),
        pltpu.make_async_copy(radial_hbm, radial, load_sem.at[5]),
        pltpu.make_async_copy(values_hbm, values, load_sem.at[6]),
    ]
    for copy in loads:
        copy.start()

    def wrap(index, count):
        return lax.bitwise_and(index, count - 1)

    barrier = pltpu.get_barrier_semaphore()

    wide = npitch // DEEP
    x, z = lax.shift_right_logical(p, 3), lax.bitwise_and(p, DEEP - 1)
    z_peers = [x * DEEP + wrap(z + step, DEEP) for step in range(1, DEEP)]
    x_peers = [wrap(p + step * DEEP, npitch) for step in range(1, wide)]
    span_peers = [wrap(s + step, nspan) for step in range(1, nspan)]
    up, down = wrap(p + 1, npitch), wrap(p + npitch - 1, npitch)
    outer, inner = wrap(s + 1, nspan), wrap(s + nspan - 1, nspan)
    greeted = [(p, peer, q) for peer in span_peers]
    greeted += [(peer, s, other) for peer in [p] + z_peers]
    greeted += [(wrap(p + far, npitch), s, q) for far in range(1, npitch)]
    for device in greeted:
        pl.semaphore_signal(barrier, inc=1, device_id=device, device_id_type=MESH)

    loads[0].wait()
    raw = flow_raw[...].astype(F32)
    flow_own[...] = jnp.concatenate([raw[:, 0, :], raw[:, 1, :]], axis=1).astype(BF16)

    pl.semaphore_wait(barrier, len(greeted))

    def send(src, dst, sems, first, device):
        return pltpu.make_async_remote_copy(
            src_ref=src,
            dst_ref=dst,
            send_sem=sems.at[first],
            recv_sem=sems.at[first + 1],
            device_id=device,
            device_id_type=MESH,
        )

    def drain(ref, sems, first):
        pltpu.make_async_copy(ref, ref, sems.at[first]).wait()
        pltpu.make_async_copy(ref, ref, sems.at[first + 1]).wait()

    for peer in span_peers:
        send(flow_own, flows.at[s], flow_sems, 0, (p, peer, q)).start()

    flows[s] = flow_own[...]

    lane = iota((8, 128), 1)
    source_lane = 127 * other
    near = lax.bitwise_and(lane + 128 - source_lane, 127)
    offset = pl.multiple_of(other * 128, 128)

    def pack(fields, tiles):
        parts = []
        for f in range(fields):
            for half in range(2):
                part = jnp.zeros((8, 128), F32)
                for i in range(cp):
                    spot = (f * 2 + half) * 16 + i
                    tile = tiles(f, i, half)
                    part = jnp.where(near == spot, pltpu.roll(tile, spot, 1) if spot else tile, part)
                parts.append(part)
        while len(parts) > 1:
            parts = [sum(parts[n : n + 2]) for n in range(0, len(parts), 2)]
        return jnp.where(q == 0, pltpu.roll(parts[0], 1, 1), parts[0])

    def halo(ref, step, count):
        pitch, span = pitch_sems.at[step], span_sems.at[step]
        return [
            send(ref.at[0:count, cp], ref.at[0:count, 0], pitch, 0, (up, s, q)),
            send(ref.at[0:count, 1], ref.at[0:count, cp + 1], pitch, 2, (down, s, q)),
            send(span_send.at[step, 0, 0:count], span_recv.at[step, 1, 0:count], span, 0, (p, inner, q)),
            send(span_send.at[step, 1, 0:count], span_recv.at[step, 0, 0:count], span, 2, (p, outer, q)),
        ]

    planes = (planes_first, planes_second)

    def spread_z(step):
        for peer in [p] + z_peers:
            send(plane_send.at[step], planes[step].at[x, z], plane_sems.at[step], 0, (peer, s, other)).start()

    def spread_x(step):
        drain(planes[step].at[0], plane_sems.at[step], 0)
        for peer in x_peers:
            send(planes[step].at[x], planes[step].at[x], plane_sems.at[step], 2, (peer, s, q)).start()

    def wait_plane(step):
        drain(planes[step].at[0 : wide - 1], plane_sems.at[step], 2)

    loads[2].wait()
    loads[3].wait()
    plane_send[0] = pack(4, lambda f, i, half: state[f, i + 1, pl.ds(half * 8, 8), pl.ds(offset, 128)])

    spread_z(0)
    first = halo(state, 0, 4)
    for copy in first[:2]:
        copy.start()

    @pl.loop(0, cp)
    def _(i):
        for f in range(4):
            span_send[0, 0, f, pl.ds(i, 1), :] = state[f, i + 1, 0:1, :]
            span_send[0, 1, f, pl.ds(i, 1), :] = state[f, i + 1, cr - 1 : cr, :]

    for copy in first[2:]:
        copy.start()

    for f in range(3):
        block = state[f, 1 : cp + 1].reshape(cp * cr, ca)
        high, low = halves(block)
        fparts[0, f] = high
        fparts[1, f] = low
    loads[1].wait()
    loads[4].wait()
    numbers = iota((256, CHUNK), 0).astype(F32).astype(BF16)
    one, zero = jnp.asarray(1, BF16), jnp.asarray(0, BF16)
    counts[...] = jnp.zeros((npitch, 1), F32)
    before = (iota((CHUNK, CHUNK), 0) < iota((CHUNK, CHUNK), 1)).astype(F32).astype(BF16)

    def sample(chunk):
        here = pl.ds(chunk * CHUNK, CHUNK)
        cell = cells[0:1, here]
        axial = lax.bitwise_and(cell, ca - 1)
        place = lax.shift_right_logical(cell, 8)
        onehot = jnp.where(numbers == axial.astype(F32).astype(BF16), one, zero)
        at_place = iota((cp * cr, CHUNK), 0) == place
        for f in range(3):
            picked = dot(fparts[0, f], onehot) + dot(fparts[1, f], onehot)
            sampled[f : f + 1, here] = jnp.sum(jnp.where(at_place, picked, 0.0), axis=0, keepdims=True)
        goal = dest[0:1, here]
        mine = iota((npitch, CHUNK), 0) == goal
        mine_f = mine.astype(F32)
        rank = dot(mine_f.astype(BF16), before) + counts[...]
        slots[0:1, here] = jnp.sum(jnp.where(mine, rank, 0.0), axis=0, keepdims=True)
        counts[...] += jnp.sum(mine_f, axis=1, keepdims=True)

    sample(0)
    sample(1)
    spread_x(0)
    sample(2)

    some = flows.at[0 : nspan - 1]
    pltpu.make_async_copy(some, some, flow_sems.at[0]).wait()
    pltpu.make_async_copy(some, some, flow_sems.at[1]).wait()

    loads[5].wait()
    kernel_rows = radial[pl.ds(pl.multiple_of(s * cr, cr), cr), :]
    smoothed = dot(kernel_rows, flows[...].reshape(nspan * cr, 2 * ca))
    speed_axial = AXIAL_SPEED * (1.0 + 0.5 * jnp.tanh(smoothed[:, :ca]))
    speed_pitch = PITCH_SPEED * jnp.tanh(smoothed[:, ca:])
    speeds[0] = speed_axial
    speeds[1] = speed_pitch
    edge = jnp.where(q == 0, speed_axial[:, ca - 1 : ca], speed_axial[:, 0:1])
    speed_send[...] = jnp.broadcast_to(edge, (cr, 128))
    speed_copy = send(speed_send, speed_recv, speed_sems, 0, (p, s, other))
    speed_copy.start()
    sample(3)

    loads[6].wait()
    hand[...] = jnp.zeros(hand.shape, F32)
    speed_parts = halves(speeds[...].reshape(2 * cr, ca))

    def pass_on(chunk):
        here = pl.ds(chunk * CHUNK, CHUNK)
        cell = cells[0:1, here]
        axial = lax.bitwise_and(cell, ca - 1)
        onehot = jnp.where(numbers == axial.astype(F32).astype(BF16), one, zero)
        picked = dot(speed_parts[0], onehot) + dot(speed_parts[1], onehot)
        radius = lax.bitwise_and(lax.shift_right_logical(cell, 8), cr - 1)
        at_radius = iota((cr, CHUNK), 0) == radius
        got = [sampled[f : f + 1, here] for f in range(3)]
        for k in range(2):
            got.append(jnp.sum(jnp.where(at_radius, picked[k * cr : (k + 1) * cr], 0.0), axis=0, keepdims=True))
        which = iota((16, CHUNK), 0)
        item = jnp.where(which >= 5, which - 5, which)
        samples = jnp.zeros((16, CHUNK), F32)
        for k in range(5):
            samples = jnp.where(item == k, got[k], samples)
        old = jnp.concatenate([values[:, here], jnp.zeros((6, CHUNK), F32)], axis=0)
        updated = jnp.where(which < 5, old + 0.5 * (samples - old), old + 0.8 * samples)
        high, low = halves(updated)
        goal = dest[0:1, here]
        odd = lax.bitwise_and(goal, 1).astype(F32)
        column = (slots[0:1, here] + 128.0 * odd).astype(BF16)
        hot = jnp.where(numbers == column, one, zero)
        pair = jnp.broadcast_to(lax.shift_right_logical(goal, 1).astype(F32), (16, CHUNK)).astype(BF16)
        pair = jnp.concatenate([pair, pair], axis=1)
        both = jnp.concatenate([high, low], axis=1)
        left = jnp.concatenate([jnp.where(pair == jnp.asarray(d, BF16), both, zero) for d in range(npitch // 2)], axis=0)
        hand[...] += dot_nt(left, jnp.concatenate([hot, hot], axis=1))

    for chunk in range(nchunk):
        pass_on(chunk)
    for d in range(npitch):
        row, column = d // 2 * 16, d % 2 * 128
        outgoing[d] = hand[row : row + 10, column : column + 128]
    for far in range(1, npitch):
        to = wrap(p + far, npitch)
        send(outgoing.at[to], landed.at[p], hand_sems, 0, (to, s, q)).start()
    landed[p] = outgoing[p]

    for copy in first:
        copy.wait()

    start_cell = map_ref[0, 0]
    facing = lax.shift_right_logical(start_cell, 4)
    shift = lax.bitwise_and(start_cell, 15)
    facing_next = lax.bitwise_and(facing + 1, npitch - 1)
    in_group = lax.bitwise_and(lane, 15)

    def facing_plane(step):
        low = planes[step][lax.shift_right_logical(facing, 3), lax.bitwise_and(facing, DEEP - 1)]
        high = planes[step][lax.shift_right_logical(facing_next, 3), lax.bitwise_and(facing_next, DEEP - 1)]
        high = pltpu.roll(high, 16, 1)
        for bit in range(4):
            moved = lax.bitwise_and(shift, 1 << bit) != 0
            low = jnp.where(moved, pltpu.roll(low, 128 - (1 << bit), 1), low)
            high = jnp.where(moved, pltpu.roll(high, 128 - (1 << bit), 1), high)
        return jnp.where(in_group + shift < 16, low, high)

    def add_to_plane(ref, first_cell, delta):
        for f in range(3):
            for half in range(2):
                for i in range(cp):
                    spot = (f * 2 + half) * 16 + i
                    where = (f, i + first_cell, pl.ds(half * 8, 8), pl.ds(offset, 128))
                    term = jnp.broadcast_to(delta[:, spot : spot + 1], (8, 128))
                    ref[where] += jnp.where(near == 0, term, 0.0)

    lanes = iota((cr, ca), 1)
    radii = iota((cr, ca), 0)
    west, east = lanes == 0, lanes == ca - 1
    hub, tip = radii == 0, radii == cr - 1
    stator = q == 0
    span_first = s == 0
    span_last = s == nspan - 1

    def around(x, inner_row, outer_row):
        out = jnp.where(tip, outer_row, pltpu.roll(x, cr - 1, 0))
        inn = jnp.where(hub, inner_row, pltpu.roll(x, 1, 0))
        right = pltpu.roll(x, ca - 1, 1)
        left = pltpu.roll(x, 1, 1)
        return out, inn, right, left

    sa = speeds[0]
    sp = speeds[1]
    no_west = jnp.logical_and(west, stator)
    no_east = jnp.logical_and(east, jnp.logical_not(stator))
    east_open = jnp.where(jnp.logical_and(east, stator), 0.0, 1.0)
    west_open = jnp.where(jnp.logical_and(west, jnp.logical_not(stator)), 0.0, 1.0)
    sa_right = jnp.where(no_east, sa, pltpu.roll(sa, ca - 1, 1))
    sa_left = jnp.where(no_west, sa, pltpu.roll(sa, 1, 1))
    w_east = 0.5 * (sa + sa_right) * east_open
    w_west = 0.5 * (sa + sa_left) * west_open
    ep, em = jnp.maximum(w_east, 0.0), jnp.minimum(w_east, 0.0)
    wp, wm = jnp.maximum(w_west, 0.0), jnp.minimum(w_west, 0.0)
    pp, pm = jnp.maximum(sp, 0.0), jnp.minimum(sp, 0.0)
    no_inner = jnp.logical_and(hub, span_first)
    no_outer = jnp.logical_and(tip, span_last)

    @pl.loop(0, cp, unroll=UNROLL)
    def _(i):
        k = state[3, i + 1]
        k_out, k_in, k_right, k_left = around(
            k, span_recv[0, 0, 3, pl.ds(i, 1), :], span_recv[0, 1, 3, pl.ds(i, 1), :]
        )
        k_right = jnp.where(no_east, k, k_right)
        k_left = jnp.where(no_west, k, k_left)
        d_up = 0.5 * (k + state[3, i + 2])
        d_down = 0.5 * (k + state[3, i])
        d_out = jnp.where(no_outer, 0.0, 0.5 * (k + k_out))
        d_in = jnp.where(no_inner, 0.0, 0.5 * (k + k_in))
        d_east = 0.5 * (k + k_right) * east_open
        d_west = 0.5 * (k + k_left) * west_open
        c_up = TIME_STEP * (d_up - pm)
        c_down = TIME_STEP * (d_down + pp)
        c_out = TIME_STEP * d_out
        c_in = TIME_STEP * d_in
        c_east = TIME_STEP * (d_east - em)
        c_west = TIME_STEP * (d_west + wp)
        center = 1.0 - (c_up + c_down + c_out + c_in) - TIME_STEP * (ep + d_east + d_west - wm)
        center = center + jnp.where(no_east, c_east, 0.0) + jnp.where(no_west, c_west, 0.0)
        coef[0, i] = center
        coef[1, i] = c_up
        coef[2, i] = c_down
        coef[3, i] = c_out
        coef[4, i] = c_in
        coef[5, i] = jnp.where(no_east, 0.0, c_east)
        coef[6, i] = jnp.where(no_west, 0.0, c_west)

    def advance(old, step, store):
        @pl.loop(0, cp, unroll=UNROLL)
        def _(i):
            c = [coef[n, i] for n in range(7)]
            for f in range(3):
                v = old[f, i + 1]
                out, inn, right, left = around(
                    v, span_recv[step, 0, f, pl.ds(i, 1), :], span_recv[step, 1, f, pl.ds(i, 1), :]
                )
                new = c[0] * v + c[1] * old[f, i + 2] + c[2] * old[f, i]
                new = new + c[3] * out + c[4] * inn + c[5] * right + c[6] * left
                store(f, i, new)

    def store_first(f, i, new):
        state2[f, i + 1] = new

    advance(state, 0, store_first)

    base = pack(3, lambda f, i, half: state2[f, i + 1, pl.ds(half * 8, 8), pl.ds(offset, 128)])
    plane_send[1] = base
    spread_z(1)

    wait_plane(0)
    speed_copy.wait()
    own = plane_send[0]
    facing_own = facing_plane(0)
    k_sum = 0.5 * (own + facing_own)
    field = lax.shift_right_logical(lane, 5)
    k_face = jnp.where(field == 0, pltpu.roll(k_sum, 32, 1), k_sum)
    k_face = jnp.where(field == 1, pltpu.roll(k_sum, 64, 1), k_face)
    k_face = jnp.where(field == 2, pltpu.roll(k_sum, 96, 1), k_face)
    speed_sum = 0.5 * (speed_send[...] + speed_recv[...])
    w_face = jnp.where(lax.bitwise_and(lane, 16) == 0, speed_sum[0:8], speed_sum[8:16])
    w_plus, w_minus = jnp.maximum(w_face, 0.0), jnp.minimum(w_face, 0.0)
    sign = jnp.where(q == 0, -TIME_STEP, TIME_STEP)

    def change(mine, theirs):
        lower = jnp.where(q == 0, mine, theirs)
        upper = jnp.where(q == 0, theirs, mine)
        return sign * (w_plus * lower + w_minus * upper - k_face * (upper - lower))

    delta = change(own, facing_own)
    add_to_plane(state2, 1, delta)

    @pl.loop(0, cp)
    def _(i):
        for f in range(3):
            span_send[1, 0, f, pl.ds(i, 1), :] = state2[f, i + 1, 0:1, :]
            span_send[1, 1, f, pl.ds(i, 1), :] = state2[f, i + 1, cr - 1 : cr, :]

    second = halo(state2, 1, 3)
    for copy in second:
        copy.start()

    spread_x(1)
    for copy in second:
        copy.wait()

    def store_second(f, i, new):
        advected_ref[f, i] = new

    advance(state2, 1, store_second)
    wait_plane(1)
    add_to_plane(advected_ref, 0, change(base + delta, facing_plane(1) - delta))

    drain(landed.at[0 : npitch - 1], hand_sems, 0)
    for d in range(npitch):
        arrived_ref[:, d * 128 : (d + 1) * 128] = landed[d]


def local(fields, diffusivity, mean_flow, radial_kernel, tracer_values, tracer_cells, tracer_dest, interface_map):
    npitch = lax.axis_size("pitch")
    nspan = lax.axis_size("span")
    tracers = tracer_values.shape[1]
    anywhere = pl.BlockSpec(memory_space=pltpu.HBM)
    vmem = pl.BlockSpec(memory_space=pltpu.VMEM)
    dma = pltpu.SemaphoreType.DMA
    return pl.pallas_call(
        functools.partial(kernel, npitch, nspan),
        out_shape=(
            pltpu.VMEM((3, 16, 16, 256), F32),
            pltpu.VMEM((10, npitch * 128), F32),
        ),
        in_specs=[anywhere] * 7 + [pl.BlockSpec(memory_space=pltpu.SMEM)],
        out_specs=(vmem, vmem),
        scratch_shapes=[
            pltpu.VMEM((4, 18, 16, 256), F32),
            pltpu.VMEM((16, 2, 256), BF16),
            pltpu.VMEM((128, nspan * 16), BF16),
            pltpu.VMEM((10, tracers), F32),
            pltpu.VMEM((1, tracers), jnp.int32),
            pltpu.VMEM((1, tracers), jnp.int32),
            pltpu.VMEM((16, 512), BF16),
            pltpu.VMEM((nspan, 16, 512), BF16),
            pltpu.VMEM((3, 18, 16, 256), F32),
            pltpu.VMEM((2, 2, 4, 16, 256), F32),
            pltpu.VMEM((2, 2, 4, 16, 256), F32),
            pltpu.VMEM((2, 8, 128), F32),
            pltpu.VMEM((npitch // DEEP, DEEP, 8, 128), F32),
            pltpu.VMEM((npitch // DEEP, DEEP, 8, 128), F32),
            pltpu.VMEM((16, 128), F32),
            pltpu.VMEM((16, 128), F32),
            pltpu.VMEM((npitch, 10, 128), F32),
            pltpu.VMEM((npitch, 10, 128), F32),
            pltpu.VMEM((2, 3, 256, 256), BF16),
            pltpu.VMEM((8, tracers), F32),
            pltpu.VMEM((8, tracers), F32),
            pltpu.VMEM((npitch, 1), F32),
            pltpu.VMEM((npitch * 8, 256), F32),
            pltpu.VMEM((2, 16, 256), F32),
            pltpu.VMEM((7, 16, 16, 256), F32),
            dma((7,)),
            dma((2,)),
            dma((2, 4)),
            dma((2, 4)),
            dma((2, 4)),
            dma((2,)),
            dma((2,)),
        ],
        compiler_params=pltpu.CompilerParams(
            collective_id=0, has_side_effects=True, vmem_limit_bytes=60 * 1024 * 1024
        ),
        name="row_step",
    )(
        fields,
        diffusivity,
        mean_flow,
        radial_kernel,
        tracer_values,
        tracer_cells.reshape(1, tracers),
        tracer_dest.reshape(1, tracers),
        interface_map,
    )


def solution(mesh):
    placed = (
        P(None, "pitch", "span", "row"),
        P("pitch", "span", "row"),
        P("span", None, "row"),
        P(),
        P(None, ("pitch", "span", "row")),
        P(("pitch", "span", "row")),
        P(("pitch", "span", "row"), None),
        P("row", "pitch"),
    )
    return jax.shard_map(
        local,
        mesh=mesh,
        in_specs=placed,
        out_specs=(P(None, "pitch", "span", "row"), P(None, ("pitch", "span", "row"))),
        check_vma=False,
    )
```
